128 devices in a mesh: lev: 64 (over z, x_hi, y, core), var: 2 (over x_lo).
Axes of the slice: x: 4 (x_hi: 2, x_lo: 2; x = x_hi * 2 + x_lo), y: 4, z: 4, core: 2. Of those that a mesh axis runs over, the one named last changes fastest.
Arguments:
- background: float32 [128, 4, 128, 1024], P('lev', 'var'), may hold values from -6 to 6
- field_ids: int32 [128, 1024], replicated, may hold values from 0 to 7
- filter_table: float32 [8, 128, 4, 2], P(None, 'lev', 'var'), may hold values from 0.02 to 0.24
- first_weight: bfloat16 [512, 1024], replicated, may hold values from -0.25 to 0.25
- first_bias: float32 [1024], replicated, may hold values from -3 to 3
- second_weight: bfloat16 [1024, 512], replicated, may hold values from -0.1875 to 0.1875
- second_bias: float32 [512], replicated, may hold values from -4 to 4
- predictor_index: int32 [512, 8], replicated, may hold values from 0 to 511
- predictor_coef: float32 [512, 8], replicated, may hold values from -3 to 3
- channel_level: int32 [512], replicated, may hold values from 0 to 127
- observed: float32 [128, 1024, 512], P(('lev', 'var')), may hold values from -10 to 10
Outputs:
- radiances: bfloat16 [128, 1024, 512], P(('lev', 'var'))
- mean_cost: float32 [], replicated
- gradient: float32 [128, 4, 128, 1024], P('lev', 'var')
The draws below stay inside these ranges and needn't reach their ends.
All inputs are finite; a program needn't handle non-finite values.
Results may differ from the reference program's by a relative error of at most 0.005.
Values may be sent and summed in bfloat16 or wider, within the bound.
A program may use at most 128 MiB of HBM per device.

```python
import jax
import jax.numpy as jnp
from jax import lax

LEVELS = 128
VARS = 4
UNITS = 1024
CHANNELS = 512
NLON = 1024
NIDS = 8
NPRED = 8
PASSES = 4
FEATURES = 512
NLAT = 128


def draw_observed(key, part):
    lat_rows = jnp.arange(NLAT, dtype=jnp.float32) / NLAT
    spread = 1.0 + 1.5 * lat_rows
    noise = jax.random.truncated_normal(key, -4.0, 4.0, (NLAT, NLON, CHANNELS), jnp.float32)
    return noise * spread[:, None, None]


def place_ends(result, rng, low, high):
    index_at = [jax.random.randint(jax.random.fold_in(rng, axis), (), 0, length) for axis, length in enumerate(result.shape)]
    widest = result.shape.index(max(result.shape))
    beside = index_at[:widest] + [(index_at[widest] + 1) % result.shape[widest]] + index_at[widest + 1:]
    return result.at[tuple(index_at)].set(low).at[tuple(beside)].set(high)


def steps_of(rng, shape, pieces, smallest, largest):
    factor_of, own = 1.0, jax.random.fold_in(rng, 6)
    for dim, blocks in pieces:
        steps = jnp.exp(jax.random.uniform(jax.random.fold_in(own, dim), (blocks,), jnp.float32, smallest / len(pieces), largest / len(pieces)))
        factor_of = factor_of * jnp.repeat(steps, shape[dim] // blocks).reshape([-1 if axis == dim else 1 for axis in range(len(shape))])
    return factor_of


def normal_values(own_key, shape, width, reach, pieces=(), kind=jnp.bfloat16):
    drawn = jax.random.normal(own_key, shape, jnp.float32) * width
    if len(pieces) > 0:
        drawn = steps_of(own_key, shape, pieces, -0.22, 0.18) * drawn
    return jnp.clip(drawn, min=-reach, max=reach).astype(kind)


def setup_inputs(seed: int = 0) -> dict:
    streams_of = jax.random.split(jax.random.key(seed), 12)
    background = normal_values(streams_of[0], (LEVELS, VARS, NLAT, NLON), 1.0, 6.0, ((0, 64), (1, 2)), jnp.float32)
    field_ids = place_ends(jax.random.randint(streams_of[1], (NLAT, NLON), 0, NIDS), jax.random.fold_in(streams_of[1], 1), 0, NIDS - 1).astype(jnp.int32)
    filter_table = jnp.clip(0.02 + 0.22 * jax.random.uniform(streams_of[2], (NIDS, LEVELS, VARS, 2), jnp.float32) ** steps_of(streams_of[2], (NIDS, LEVELS, VARS, 2), ((1, 64), (2, 2)), -0.2, 0.2), 0.02, 0.24)
    first_weight = normal_values(streams_of[3], (FEATURES, UNITS), FEATURES ** -0.5, 0.25)
    first_bias = normal_values(streams_of[4], (UNITS,), 0.5, 3.0, (), jnp.float32)
    second_weight = normal_values(streams_of[5], (UNITS, CHANNELS), UNITS ** -0.5, 0.1875)
    second_bias = normal_values(streams_of[6], (CHANNELS,), 1.0, 4.0, (), jnp.float32)
    predictor_index = place_ends(jax.random.randint(streams_of[7], (CHANNELS, NPRED), 0, FEATURES), jax.random.fold_in(streams_of[7], 1), 0, FEATURES - 1).astype(jnp.int32)
    predictor_coef = normal_values(streams_of[8], (CHANNELS, NPRED), 0.5, 3.0, (), jnp.float32)
    channel_level = place_ends(jax.random.randint(streams_of[9], (CHANNELS,), 0, LEVELS), jax.random.fold_in(streams_of[9], 1), 0, LEVELS - 1).astype(jnp.int32)
    observed = draw_observed(jax.random.fold_in(streams_of[11], 71), 0)
    return {"background": background, "field_ids": field_ids, "filter_table": filter_table, "first_weight": first_weight, "first_bias": first_bias, "second_weight": second_weight, "second_bias": second_bias, "predictor_index": predictor_index, "predictor_coef": predictor_coef, "channel_level": channel_level, "observed": observed}


def lat_second(plane):
    widths = [(0, 0)] * (plane.ndim - 2) + [(1, 1), (0, 0)]
    padded = jnp.pad(plane, widths)
    return padded[..., 2:, :] + padded[..., :-2, :] - 2.0 * plane


def lon_second(plane):
    return jnp.roll(plane, 1, plane.ndim - 1) + jnp.roll(plane, -1, plane.ndim - 1) - 2.0 * plane


def coefficient_fields(field_ids, coef_table):
    shape = coef_table.shape[1:-1] + field_ids.shape
    lat_coef = jnp.zeros(shape, jnp.float32)
    lon_coef = jnp.zeros(shape, jnp.float32)
    for ident in range(coef_table.shape[0]):
        matched = field_ids == ident
        lat_coef = jnp.where(matched, coef_table[ident, ..., 0][..., None, None], lat_coef)
        lon_coef = jnp.where(matched, coef_table[ident, ..., 1][..., None, None], lon_coef)
    return lat_coef, lon_coef


def selection(predictor_index, predictor_coef, channel_level, features):
    feature_ids = jnp.arange(features, dtype=jnp.int32)
    picked = jnp.sum(jnp.where(feature_ids[:, None, None] == predictor_index[None], predictor_coef[None], jnp.float32(0.0)), axis=2)
    peak_term = jnp.where(feature_ids[:, None] // VARS == channel_level[None, :], jnp.float32(1.0), jnp.float32(0.0))
    return picked + peak_term


def reference(background, field_ids, filter_table, first_weight, first_bias, second_weight, second_bias, predictor_index, predictor_coef, channel_level, observed):
    tables = jnp.moveaxis(filter_table, 1, 0)

    def forward_level(pair):
        state, coef_table = pair
        lat_coef, lon_coef = coefficient_fields(field_ids, coef_table)
        for number in range(PASSES):
            state = state + lat_coef * lat_second(state) + lon_coef * lon_second(state)
        return state.astype(jnp.bfloat16)

    filtered = lax.map(forward_level, (background, tables))
    columns = filtered.transpose(2, 3, 0, 1).reshape(NLAT, NLON, LEVELS * VARS)
    selector = selection(predictor_index, predictor_coef, channel_level, LEVELS * VARS)

    def column_row(pair):
        inputs, wanted = pair
        pre = jnp.dot(inputs, first_weight, preferred_element_type=jnp.float32) + first_bias
        active = jnp.tanh(pre)
        evolved = jnp.dot(active.astype(jnp.bfloat16), second_weight, preferred_element_type=jnp.float32) + second_bias
        evolved = evolved + jnp.dot(inputs.astype(jnp.float32), selector, precision=lax.Precision.HIGHEST)
        depart = evolved - wanted
        cost_row = jnp.sum(0.5 * depart * depart)
        back_active = jnp.dot(depart.astype(jnp.bfloat16), second_weight.T, preferred_element_type=jnp.float32)
        back_pre = (back_active * (1.0 - active * active)).astype(jnp.bfloat16)
        column_grad = jnp.dot(back_pre, first_weight.T, preferred_element_type=jnp.float32)
        column_grad = column_grad + jnp.dot(depart, selector.T, precision=lax.Precision.HIGHEST)
        return evolved.astype(jnp.bfloat16), column_grad.astype(jnp.bfloat16), cost_row

    radiances, column_grad, cost_rows = lax.map(column_row, (columns, observed))
    mean_cost = jnp.sum(cost_rows) / (NLAT * NLON * CHANNELS)
    adjoint_in = column_grad.reshape(NLAT, NLON, LEVELS, VARS).transpose(2, 3, 0, 1)

    def adjoint_level(pair):
        incoming, coef_table = pair
        lat_coef, lon_coef = coefficient_fields(field_ids, coef_table)
        adjoint = incoming.astype(jnp.float32)
        for number in range(PASSES):
            adjoint = adjoint + lat_second(lat_coef * adjoint) + lon_second(lon_coef * adjoint)
        return adjoint

    gradient = lax.map(adjoint_level, (adjoint_in, tables))
    return radiances, mean_cost, gradient
```

```python
import functools

import jax
import jax.numpy as jnp
from jax import lax
from jax.experimental import pallas as pl
from jax.experimental.pallas import tpu as pltpu
from jax.sharding import PartitionSpec as P

PASSES = 4
DEVICES = 128
PLANES = 4
LAT, LON = 128, 1024
STEP = 16
LANES = 128
STRIPS = 1024 // LANES
NQ = 4
CHUNKS = LON // (LANES * NQ)
ROWS = PLANES * NQ
COLS = LANES * NQ
FEATURES, UNITS, CHANNELS = 512, 1024, 512
MESH = pl.DeviceIdType.MESH
F32, BF16 = jnp.float32, jnp.bfloat16


def offset_of(number):
    return (number // 32, (number // 8) % 4, (number // 2) % 4, number % 2)


def hops_of(number):
    return sum(min(part, 4 - part) for part in offset_of(number)[:3])


ORDER = sorted(range(1, DEVICES), key=lambda n: (-hops_of(n), (n * 73 + 19) * 2654435761 % 4294967291))


def targets():
    lev, var = lax.axis_index("lev"), lax.axis_index("var")
    z, high, y, core = lev // 16, (lev // 8) % 2, (lev // 2) % 4, lev % 2
    x = high * 2 + var
    zs = [((z + d) % 4) * 16 for d in range(4)]
    ys = [((y + d) % 4) * 2 for d in range(4)]
    xs = [(x + d) % 4 for d in range(4)]
    cores = [(core + d) % 2 for d in range(2)]
    zy = [[a + b for b in ys] for a in zs]
    xc = [[(a // 2) * 8 + b for b in cores] for a in xs]
    low = [a % 2 for a in xs]
    found = []
    for number in ORDER:
        dz, dy, dx, dc = offset_of(number)
        found.append((zy[dz][dy] + xc[dx][dc], low[dx]))
    return lev * 2 + var, found


def scatter_rows(where, start, step, values):
    where[pl.ds(start, 8, stride=step), :] = values


def gather_rows(strips, k):
    return jnp.concatenate([strip[pl.ds(k, 8, stride=STEP), :] for strip in strips], axis=1)


def neighbours(held, k):
    sub = lax.broadcasted_iota(jnp.int32, (8, LON), 0)
    if k < STEP - 1:
        above = held[k + 1]
    else:
        above = jnp.where(sub == 7, 0.0, pltpu.roll(held[0], 7, 0))
    if k > 0:
        below = held[k - 1]
    else:
        below = jnp.where(sub == 0, 0.0, pltpu.roll(held[STEP - 1], 1, 0))
    return above, below


def sideways(value):
    return pltpu.roll(value, 1, 1) + pltpu.roll(value, LON - 1, 1)


def forward_kernel(
    grid_ref, ids_ref, table_ref, w1_ref, b1_ref, w2_ref, b2_ref, index_ref, coef_ref, level_ref, seen_ref,
    back_ref, lat_ref, lon_ref, rad_ref, cost_ref,
    planes, ids, flip, mixed, send, got, send_back, w1raw, w1, w2, obs, wide, sel_hi, sel_lo, turned,
    active_ref, total,
    grid_sem, ids_sem, w1_sem, w2_sem, obs_sem, own_sem, out1, in1, out2, in2, out3, in3,
):
    me, peers = targets()
    barrier = pltpu.get_barrier_semaphore()
    for lev, var in peers:
        pl.semaphore_signal(barrier, 1, device_id=(lev, var), device_id_type=MESH)
    strips = [pl.ds(j * LANES, LANES) for j in range(STRIPS)]
    ids_copies = [pltpu.make_async_copy(ids_ref.at[:, s], ids.at[j], ids_sem.at[j]) for j, s in enumerate(strips)]
    for copy in ids_copies:
        copy.start()
    grid_copies = [
        pltpu.make_async_copy(grid_ref.at[p, :, s], planes.at[p, j], grid_sem.at[p, j])
        for p in range(PLANES)
        for j, s in enumerate(strips)
    ]
    for copy in grid_copies:
        copy.start()
    w1_copy = pltpu.make_async_copy(w1_ref, w1raw, w1_sem)
    w2_copy = pltpu.make_async_copy(w2_ref, w2, w2_sem)
    obs_copy = pltpu.make_async_copy(seen_ref, obs, obs_sem)
    w1_copy.start()
    w2_copy.start()
    obs_copy.start()

    for copy in ids_copies:
        copy.wait()

    @pl.loop(0, STEP)
    def _(k):
        field = gather_rows([ids.at[j] for j in range(STRIPS)], k)
        bits = [(field & (1 << n)) != 0 for n in range(3)]
        for p in range(PLANES):
            for axis, where in ((0, lat_ref), (1, lon_ref)):
                level = [table_ref[n * 8 + p * 2 + axis] for n in range(8)]
                for bit in bits:
                    level = [jnp.where(bit, level[2 * n + 1], level[2 * n]) for n in range(len(level) // 2)]
                where[p, k] = level[0]

    for copy in grid_copies:
        copy.wait()

    @pl.loop(0, PLANES)
    def _(p):
        for k in range(STEP):
            flip[0, k] = gather_rows([planes.at[p, j] for j in range(STRIPS)], k)
        for number in range(PASSES):
            held = flip.at[number % 2]
            for k in range(STEP):
                above, below = neighbours(held, k)
                value = held[k]
                twice = value + value
                value = (
                    value
                    + lat_ref[p, k] * (above + below - twice)
                    + lon_ref[p, k] * (sideways(value) - twice)
                )
                if number < PASSES - 1:
                    flip[1 - number % 2, k] = value
                else:
                    for c in range(CHUNKS):
                        for q in range(NQ):
                            at = (c * NQ + q) * LANES
                            scatter_rows(
                                mixed.at[c], k * ROWS + p * NQ + q, STEP * ROWS, value[:, at : at + LANES]
                            )

    @pl.loop(0, CHUNKS)
    def _(c):
        @pl.loop(0, DEVICES, unroll=4)
        def _(d):
            send[c, d] = mixed[c, pl.ds(pl.multiple_of(d * ROWS, ROWS), ROWS), :].astype(BF16)

    pl.semaphore_wait(barrier, DEVICES - 1)

    @pl.loop(0, CHUNKS)
    def _(c):
        for lev, var in peers:
            pltpu.make_async_remote_copy(
                send.at[c, lev * 2 + var], got.at[c, me], out1.at[c], in1.at[c],
                device_id=(lev, var), device_id_type=MESH,
            ).start()
        pltpu.make_async_copy(send.at[c, me], got.at[c, me], own_sem.at[c]).start()

    row = lax.broadcasted_iota(jnp.int32, (CHANNELS, FEATURES), 1)
    feature = (row % 64) * 8 + (row // 256) * 4 + ((row // 64) % 2) * 2 + (row // 128) % 2
    picks = jnp.where(feature // 4 == level_ref[...], 1.0, 0.0).astype(F32)
    for n in range(8):
        picks = picks + jnp.where(feature == index_ref[:, n : n + 1], coef_ref[:, n : n + 1], 0.0)
    wide[0:FEATURES, 0:CHANNELS] = picks.T
    picks = wide[0:FEATURES, 0:CHANNELS]
    high = picks.astype(BF16)
    sel_hi[...] = high
    sel_lo[...] = (picks - high.astype(F32)).astype(BF16)
    w1_copy.wait()
    for part in range(UNITS // LANES):
        turned[0:FEATURES, :] = w1raw[:, part * LANES : (part + 1) * LANES].astype(F32)
        for s in range(8):
            block = turned[pl.ds(s, 64, stride=8), :]
            at = ((s // 4) * 2 + s % 2) * LANES + ((s // 2) % 2) * 64
            w1[at : at + 64, part * LANES : (part + 1) * LANES] = block.astype(BF16)
    w2_copy.wait()
    obs_copy.wait()
    total[...] = jnp.zeros_like(total)

    @pl.loop(0, CHUNKS)
    def _(c):
        pltpu.make_async_copy(send.at[c, me], got.at[c, me], own_sem.at[c]).wait()
        others = pl.ds(0, DEVICES - 1)
        pltpu.make_async_copy(got.at[c, others], got.at[c, others], in1.at[c]).wait()

        @pl.loop(0, DEVICES, unroll=4)
        def _(d):
            mixed[c, pl.ds(pl.multiple_of(d * ROWS, ROWS), ROWS), :] = got[c, d].astype(F32)

        for q in range(NQ):
            for p in range(PLANES):
                for var in range(2):
                    block = mixed[c, pl.ds(var * ROWS + p * NQ + q, 64, stride=2 * ROWS), :]
                    turned[p * LANES + var * 64 : p * LANES + var * 64 + 64, :] = block
            columns = turned[...].T.astype(BF16)
            first = pl.multiple_of(c * COLS + q * LANES, LANES)
            spot = pl.ds(first, LANES)
            active = jnp.tanh(jnp.dot(columns, w1[...], preferred_element_type=F32) + b1_ref[...])
            evolved = jnp.dot(active.astype(BF16), w2[...], preferred_element_type=F32) + b2_ref[...]
            evolved = evolved + jnp.dot(columns, sel_hi[...], preferred_element_type=F32)
            evolved = evolved + jnp.dot(columns, sel_lo[...], preferred_element_type=F32)
            rad_ref[spot, :] = evolved.astype(BF16)
            depart = evolved - obs[spot, :]
            total[...] += jnp.sum((depart * depart).reshape(LANES // 8, 8, CHANNELS), axis=0)
            depart_hi = depart.astype(BF16)
            depart_lo = (depart - depart_hi.astype(F32)).astype(BF16)
            turn = (((1,), (1,)), ((), ()))
            pull = lax.dot_general(depart_hi, w2[...], turn, preferred_element_type=F32)
            pull = (pull * (1.0 - active * active)).astype(BF16)
            slope = lax.dot_general(w1[...], pull, turn, preferred_element_type=F32)
            slope = slope + lax.dot_general(sel_hi[...], depart_hi, turn, preferred_element_type=F32)
            slope = slope + lax.dot_general(sel_lo[...], depart_hi, turn, preferred_element_type=F32)
            slope = slope + lax.dot_general(sel_hi[...], depart_lo, turn, preferred_element_type=F32)
            for p in range(PLANES):
                for var in range(2):
                    at = p * LANES + var * 64
                    mixed[c, pl.ds(var * ROWS + p * NQ + q, 64, stride=2 * ROWS), :] = slope[at : at + 64]

        @pl.loop(0, DEVICES, unroll=4)
        def _(d):
            send_back[c, d] = mixed[c, pl.ds(pl.multiple_of(d * ROWS, ROWS), ROWS), :].astype(BF16)

        for lev, var in peers:
            pltpu.make_async_remote_copy(
                send_back.at[c, lev * 2 + var], back_ref.at[c, me], out2.at[c], in2.at[c],
                device_id=(lev, var), device_id_type=MESH,
            ).start()
        pltpu.make_async_copy(send_back.at[c, me], back_ref.at[c, me], own_sem.at[c]).start()

    summed = jnp.sum(total[...], axis=0, keepdims=True)
    summed = sum(summed[:, n * LANES : (n + 1) * LANES] for n in range(CHANNELS // LANES))
    cost_ref[me] = summed
    for lev, var in peers:
        pltpu.make_async_remote_copy(
            cost_ref.at[me], cost_ref.at[me], out3, in3, device_id=(lev, var), device_id_type=MESH
        ).start()
    others = pl.ds(0, DEVICES - 1)
    for c in range(CHUNKS):
        pltpu.make_async_copy(send.at[c, others], send.at[c, others], out1.at[c]).wait()
        pltpu.make_async_copy(send_back.at[c, me], back_ref.at[c, me], own_sem.at[c]).wait()
        pltpu.make_async_copy(send_back.at[c, others], send_back.at[c, others], out2.at[c]).wait()
        pltpu.make_async_copy(back_ref.at[c, others], back_ref.at[c, others], in2.at[c]).wait()
    pltpu.make_async_copy(cost_ref.at[others], cost_ref.at[others], out3).wait()
    pltpu.make_async_copy(cost_ref.at[others], cost_ref.at[others], in3).wait()


def adjoint_kernel(
    back_ref, lat_ref, lon_ref, rad_ref, cost_ref,
    grad_ref, rad_out, mean_ref,
    mixed, flip, staged, rad_sem, grad_sem,
):
    rad_copy = pltpu.make_async_copy(rad_ref, rad_out, rad_sem)
    rad_copy.start()

    def leaving(p, j):
        strip = pl.ds(j * LANES, LANES)
        return pltpu.make_async_copy(staged.at[p, j], grad_ref.at[p, :, strip], grad_sem.at[p, j])

    for c in range(CHUNKS):

        @pl.loop(0, DEVICES, unroll=4)
        def _(d):
            mixed[c, pl.ds(pl.multiple_of(d * ROWS, ROWS), ROWS), :] = back_ref[c, d].astype(F32)

    @pl.loop(0, PLANES)
    def _(p):
        for k in range(STEP):
            pieces = [
                mixed[c, pl.ds(k * ROWS + p * NQ + q, 8, stride=STEP * ROWS), :]
                for c in range(CHUNKS)
                for q in range(NQ)
            ]
            flip[0, k] = jnp.concatenate(pieces, axis=1)
        for number in range(PASSES):
            held = flip.at[number % 2]
            sub = lax.broadcasted_iota(jnp.int32, (8, LON), 0)
            first = lat_ref[p, 0] * held[0]
            last = lat_ref[p, STEP - 1] * held[STEP - 1]
            below = jnp.where(sub == 0, 0.0, pltpu.roll(last, 1, 0))
            here = first
            for k in range(STEP):
                if k < STEP - 1:
                    above = lat_ref[p, k + 1] * held[k + 1]
                else:
                    above = jnp.where(sub == 7, 0.0, pltpu.roll(first, 7, 0))
                value = held[k]
                along = lon_ref[p, k] * value
                value = value + (above + below - (here + here)) + (sideways(along) - (along + along))
                below, here = here, above
                if number < PASSES - 1:
                    flip[1 - number % 2, k] = value
                else:
                    for j in range(STRIPS):
                        staged[p, j, pl.ds(k, 8, stride=STEP), :] = value[:, j * LANES : (j + 1) * LANES]
        for j in range(STRIPS):
            leaving(p, j).start()

    mean_ref[0, 0] = jnp.sum(cost_ref[...]) * (0.5 / (LAT * LON * CHANNELS))
    for p in range(PLANES):
        for j in range(STRIPS):
            leaving(p, j).wait()
    rad_copy.wait()


def shards(
    background, field_ids, filter_table, first_weight, first_bias, second_weight, second_bias,
    predictor_index, predictor_coef, channel_level, observed,
):
    vmem = pl.BlockSpec(memory_space=pltpu.VMEM)
    smem = pl.BlockSpec(memory_space=pltpu.SMEM)
    anywhere = pl.BlockSpec(memory_space=pl.ANY)
    dma = pltpu.SemaphoreType.DMA
    message = (CHUNKS, DEVICES, ROWS, LANES)
    coefs = jax.ShapeDtypeStruct((PLANES, STEP, 8, LON), F32)
    outcome = pl.pallas_call(
        forward_kernel,
        out_shape=(
            jax.ShapeDtypeStruct(message, BF16),
            coefs,
            coefs,
            jax.ShapeDtypeStruct((LON, CHANNELS), BF16),
            jax.ShapeDtypeStruct((DEVICES, 1, LANES), F32),
        ),
        in_specs=[anywhere, anywhere, smem, anywhere, vmem, anywhere, vmem, vmem, vmem, vmem, anywhere],
        out_specs=[vmem] * 5,
        scratch_shapes=[
            pltpu.VMEM((PLANES, STRIPS, LAT, LANES), F32),
            pltpu.VMEM((STRIPS, LAT, LANES), jnp.int32),
            pltpu.VMEM((2, STEP, 8, LON), F32),
            pltpu.VMEM((CHUNKS, DEVICES * ROWS, LANES), F32),
            pltpu.VMEM(message, BF16),
            pltpu.VMEM(message, BF16),
            pltpu.VMEM(message, BF16),
            pltpu.VMEM((FEATURES, UNITS), BF16),
            pltpu.VMEM((FEATURES, UNITS), BF16),
            pltpu.VMEM((UNITS, CHANNELS), BF16),
            pltpu.VMEM((LON, CHANNELS), F32),
            pltpu.VMEM((FEATURES, CHANNELS), F32),
            pltpu.VMEM((FEATURES, CHANNELS), BF16),
            pltpu.VMEM((FEATURES, CHANNELS), BF16),
            pltpu.VMEM((FEATURES, LANES), F32),
            pltpu.VMEM((8, LANES), F32),
            pltpu.VMEM((8, CHANNELS), F32),
            dma((PLANES, STRIPS)), dma((STRIPS,)), dma, dma, dma,
            dma((CHUNKS,)), dma((CHUNKS,)), dma((CHUNKS,)), dma((CHUNKS,)), dma((CHUNKS,)), dma, dma,
        ],
        compiler_params=pltpu.CompilerParams(
            collective_id=0, has_side_effects=True, vmem_limit_bytes=40 * 1024 * 1024
        ),
    )(
        background.reshape(PLANES, LAT, LON),
        field_ids,
        filter_table.reshape(64),
        first_weight,
        first_bias.reshape(1, UNITS),
        second_weight,
        second_bias.reshape(1, CHANNELS),
        predictor_index,
        predictor_coef,
        channel_level.reshape(CHANNELS, 1),
        observed.reshape(LON, CHANNELS),
    )
    gradient, radiances, mean_cost = pl.pallas_call(
        adjoint_kernel,
        out_shape=(
            jax.ShapeDtypeStruct((PLANES, LAT, LON), F32),
            jax.ShapeDtypeStruct((LON, CHANNELS), BF16),
            jax.ShapeDtypeStruct((1, 1), F32),
        ),
        in_specs=[vmem] * 5,
        out_specs=[anywhere, anywhere, smem],
        scratch_shapes=[
            pltpu.VMEM((CHUNKS, DEVICES * ROWS, LANES), F32),
            pltpu.VMEM((2, STEP, 8, LON), F32),
            pltpu.VMEM((PLANES, STRIPS, LAT, LANES), F32),
            dma,
            dma((PLANES, STRIPS)),
        ],
        compiler_params=pltpu.CompilerParams(vmem_limit_bytes=24 * 1024 * 1024),
    )(*outcome)
    return (
        radiances.reshape(1, LON, CHANNELS),
        mean_cost.reshape(()),
        gradient.reshape(2, 2, LAT, LON),
    )


def solution(mesh):
    placed = (
        P("lev", "var", None, None), P(), P(None, "lev", "var", None), P(), P(), P(), P(), P(), P(), P(),
        P(("lev", "var"), None, None),
    )
    return jax.shard_map(
        shards,
        mesh=mesh,
        in_specs=placed,
        out_specs=(P(("lev", "var"), None, None), P(), P("lev", "var", None, None)),
        check_vma=False,
    )
```

```python
import functools

import jax
import jax.numpy as jnp
from jax import lax
from jax.experimental import pallas as pl
from jax.experimental.pallas import tpu as pltpu
from jax.sharding import PartitionSpec as P

PASSES = 4
DEVICES = 128
PLANES = 4
FIELDS = 8
TERMS = 8
LAT, LON = 128, 1024
STEP = 16
LANES = 128
STRIPS = 1024 // LANES
NQ = 2
CHUNKS = LON // (LANES * NQ)
ROWS = PLANES * NQ
COLS = LANES * NQ
BLOCK = 256
FEATURES, UNITS, CHANNELS = 512, 1024, 512
MESH = pl.DeviceIdType.MESH
F32, BF16 = jnp.float32, jnp.bfloat16


def offset_of(number):
    return (number // 32, (number // 8) % 4, (number // 2) % 4, number % 2)


def hops_of(number):
    return sum(min(part, 4 - part) for part in offset_of(number)[:3])


ORDER = sorted(range(1, DEVICES), key=lambda n: (-hops_of(n), (n * 73 + 19) * 2654435761 % 4294967291))


def targets():
    lev, var = lax.axis_index("lev"), lax.axis_index("var")
    z, high, y, core = lev // 16, (lev // 8) % 2, (lev // 2) % 4, lev % 2
    x = high * 2 + var
    zs = [((z + d) % 4) * 16 for d in range(4)]
    ys = [((y + d) % 4) * 2 for d in range(4)]
    xs = [(x + d) % 4 for d in range(4)]
    cores = [(core + d) % 2 for d in range(2)]
    zy = [[a + b for b in ys] for a in zs]
    xc = [[(a // 2) * 8 + b for b in cores] for a in xs]
    low = [a % 2 for a in xs]
    found = []
    for number in ORDER:
        dz, dy, dx, dc = offset_of(number)
        found.append((zy[dz][dy] + xc[dx][dc], low[dx]))
    return lev * 2 + var, found


def scatter_rows(where, start, step, values):
    where[pl.ds(start, 8, stride=step), :] = values


def gather_rows(strips, k):
    return jnp.concatenate([strip[pl.ds(k, 8, stride=STEP), :] for strip in strips], axis=1)


def neighbours(held, k):
    sub = lax.broadcasted_iota(jnp.int32, (8, LON), 0)
    if k < STEP - 1:
        above = held[k + 1]
    else:
        above = jnp.where(sub == 7, 0.0, pltpu.roll(held[0], 7, 0))
    if k > 0:
        below = held[k - 1]
    else:
        below = jnp.where(sub == 0, 0.0, pltpu.roll(held[STEP - 1], 1, 0))
    return above, below


def sideways(value):
    return pltpu.roll(value, 1, 1) + pltpu.roll(value, LON - 1, 1)


def coefficient_fields(ids, table_ref, lat_ref, lon_ref):
    @pl.loop(0, STEP)
    def _(k):
        field = gather_rows([ids.at[j] for j in range(STRIPS)], k)
        bits = [(field & (1 << n)) != 0 for n in range(3)]
        for p in range(PLANES):
            for axis, where in ((0, lat_ref), (1, lon_ref)):
                level = [table_ref[p, axis, n] for n in range(FIELDS)]
                for bit in bits:
                    level = [jnp.where(bit, level[2 * n + 1], level[2 * n]) for n in range(len(level) // 2)]
                where[p, k] = level[0]


def smooth(planes, flip, lat_ref, lon_ref, mixed):
    @pl.loop(0, PLANES)
    def _(p):
        for k in range(STEP):
            flip[0, k] = gather_rows([planes.at[p, j] for j in range(STRIPS)], k)
        for number in range(PASSES):
            held = flip.at[number % 2]
            for k in range(STEP):
                above, below = neighbours(held, k)
                value = held[k]
                twice = value + value
                value = (
                    value
                    + lat_ref[p, k] * (above + below - twice)
                    + lon_ref[p, k] * (sideways(value) - twice)
                )
                if number < PASSES - 1:
                    flip[1 - number % 2, k] = value
                else:
                    for c in range(CHUNKS):
                        for q in range(NQ):
                            at = (c * NQ + q) * LANES
                            scatter_rows(
                                mixed.at[c], k * ROWS + p * NQ + q, STEP * ROWS, value[:, at : at + LANES]
                            )


def narrow(mixed, c, send):
    @pl.loop(0, DEVICES, unroll=4)
    def _(d):
        send[c, d] = mixed[c, pl.ds(pl.multiple_of(d * ROWS, ROWS), ROWS), :].astype(BF16)


def widen(got, c, mixed):
    @pl.loop(0, DEVICES, unroll=4)
    def _(d):
        mixed[c, pl.ds(pl.multiple_of(d * ROWS, ROWS), ROWS), :] = got[c, d].astype(F32)


def selection(index_ref, coef_ref, level_ref, sel_hi, sel_lo):
    @pl.loop(0, FEATURES // 64)
    def _(group):
        row = lax.broadcasted_iota(jnp.int32, (64, CHANNELS), 0)
        feature = row * 8 + (group // 4) * 4 + (group % 2) * 2 + (group // 2) % 2
        picks = jnp.where(feature // 4 == level_ref[...], 1.0, 0.0).astype(F32)
        for n in range(TERMS):
            picks = picks + jnp.where(feature == index_ref[n : n + 1, :], coef_ref[n : n + 1, :], 0.0)
        high = picks.astype(BF16)
        at = pl.ds(pl.multiple_of(group * 64, 64), 64)
        sel_hi[at, :] = high
        sel_lo[at, :] = (picks - high.astype(F32)).astype(BF16)


def regroup(w1raw, turned, w1):
    for part in range(UNITS // LANES):
        turned[...] = w1raw[:, part * LANES : (part + 1) * LANES].astype(F32)
        for s in range(8):
            block = turned[pl.ds(s, 64, stride=8), :]
            at = ((s // 4) * 2 + s % 2) * LANES + ((s // 2) % 2) * 64
            w1[at : at + 64, part * LANES : (part + 1) * LANES] = block.astype(BF16)


def network(c, mixed, turned, w1, b1_ref, w2, b2_ref, sel_hi, sel_lo, obs, rad_ref, total):
    for part in range(COLS // BLOCK):
        tiles = range(part * BLOCK // LANES, (part + 1) * BLOCK // LANES)
        for n, q in enumerate(tiles):
            for p in range(PLANES):
                for var in range(2):
                    block = mixed[c, pl.ds(var * ROWS + p * NQ + q, 64, stride=2 * ROWS), :]
                    at = p * LANES + var * 64
                    turned[at : at + 64, n * LANES : (n + 1) * LANES] = block
        columns = turned[...].T.astype(BF16)
        spot = pl.ds(pl.multiple_of(c * COLS + part * BLOCK, BLOCK), BLOCK)
        active = jnp.tanh(jnp.dot(columns, w1[...], preferred_element_type=F32) + b1_ref[...])
        evolved = jnp.dot(active.astype(BF16), w2[...], preferred_element_type=F32) + b2_ref[...]
        evolved = evolved + jnp.dot(columns, sel_hi[...], preferred_element_type=F32)
        evolved = evolved + jnp.dot(columns, sel_lo[...], preferred_element_type=F32)
        rad_ref[spot, :] = evolved.astype(BF16)
        depart = evolved - obs[spot, :]
        total[...] += jnp.sum((depart * depart).reshape(BLOCK // 8, 8, CHANNELS), axis=0)
        depart_hi = depart.astype(BF16)
        depart_lo = (depart - depart_hi.astype(F32)).astype(BF16)
        turn = (((1,), (1,)), ((), ()))
        pull = lax.dot_general(depart_hi, w2[...], turn, preferred_element_type=F32)
        pull = (pull * (1.0 - active * active)).astype(BF16)
        slope = lax.dot_general(w1[...], pull, turn, preferred_element_type=F32)
        slope = slope + lax.dot_general(sel_hi[...], depart_hi, turn, preferred_element_type=F32)
        slope = slope + lax.dot_general(sel_lo[...], depart_hi, turn, preferred_element_type=F32)
        slope = slope + lax.dot_general(sel_hi[...], depart_lo, turn, preferred_element_type=F32)
        for n, q in enumerate(tiles):
            for p in range(PLANES):
                for var in range(2):
                    at = p * LANES + var * 64
                    block = slope[at : at + 64, n * LANES : (n + 1) * LANES]
                    mixed[c, pl.ds(var * ROWS + p * NQ + q, 64, stride=2 * ROWS), :] = block


def forward_kernel(
    grid_ref, ids_ref, table_hbm, w1_ref, b1_hbm, w2_ref, b2_hbm, index_hbm, coef_hbm, level_hbm, seen_ref,
    back_ref, lat_ref, lon_ref, rad_ref, cost_ref,
    planes, ids, flip, mixed, send, got, send_back, w1raw, w1, w2, obs, sel_hi, sel_lo, strip, turned,
    table_ref, b1_ref, b2_ref, index_ref, coef_ref, level_ref, total,
    grid_sem, ids_sem, table_sem, small_sem, w1_sem, w2_sem, obs_sem, own_sem, out1, in1, out2, in2, out3, in3,
):
    me, peers = targets()
    barrier = pltpu.get_barrier_semaphore()
    for lev, var in peers:
        pl.semaphore_signal(barrier, 1, device_id=(lev, var), device_id_type=MESH)
    strips = [pl.ds(j * LANES, LANES) for j in range(STRIPS)]
    ids_copies = [pltpu.make_async_copy(ids_ref.at[:, s], ids.at[j], ids_sem.at[j]) for j, s in enumerate(strips)]
    for copy in ids_copies:
        copy.start()
    table_copy = pltpu.make_async_copy(table_hbm, table_ref, table_sem)
    table_copy.start()
    grid_copies = [
        pltpu.make_async_copy(grid_ref.at[p, :, s], planes.at[p, j], grid_sem.at[p, j])
        for p in range(PLANES)
        for j, s in enumerate(strips)
    ]
    for copy in grid_copies:
        copy.start()
    w1_copy = pltpu.make_async_copy(w1_ref, w1raw, w1_sem)
    w2_copy = pltpu.make_async_copy(w2_ref, w2, w2_sem)
    obs_copy = pltpu.make_async_copy(seen_ref, obs, obs_sem)
    small_copies = [
        pltpu.make_async_copy(here, there, small_sem.at[n])
        for n, (here, there) in enumerate(
            (
                (index_hbm, index_ref), (coef_hbm, coef_ref), (level_hbm, level_ref), (b1_hbm, b1_ref), (b2_hbm, b2_ref)
            )
        )
    ]
    for copy in small_copies:
        copy.start()
    w1_copy.start()
    w2_copy.start()
    obs_copy.start()

    for copy in ids_copies:
        copy.wait()
    table_copy.wait()
    coefficient_fields(ids, table_ref, lat_ref, lon_ref)
    for copy in grid_copies:
        copy.wait()

    smooth(planes, flip, lat_ref, lon_ref, mixed)
    for c in range(CHUNKS):
        narrow(mixed, c, send)

    pl.semaphore_wait(barrier, DEVICES - 1)

    @pl.loop(0, CHUNKS)
    def _(c):
        for lev, var in peers:
            pltpu.make_async_remote_copy(
                send.at[c, lev * 2 + var], got.at[c, me], out1.at[c], in1.at[c],
                device_id=(lev, var), device_id_type=MESH,
            ).start()
        pltpu.make_async_copy(send.at[c, me], got.at[c, me], own_sem.at[c]).start()

    for copy in small_copies:
        copy.wait()
    selection(index_ref, coef_ref, level_ref, sel_hi, sel_lo)
    w1_copy.wait()
    regroup(w1raw, strip, w1)
    w2_copy.wait()
    obs_copy.wait()
    total[...] = jnp.zeros_like(total)

    @pl.loop(0, CHUNKS)
    def _(c):
        pltpu.make_async_copy(send.at[c, me], got.at[c, me], own_sem.at[c]).wait()
        others = pl.ds(0, DEVICES - 1)
        pltpu.make_async_copy(got.at[c, others], got.at[c, others], in1.at[c]).wait()

        widen(got, c, mixed)
        network(c, mixed, turned, w1, b1_ref, w2, b2_ref, sel_hi, sel_lo, obs, rad_ref, total)
        narrow(mixed, c, send_back)
        for lev, var in peers:
            pltpu.make_async_remote_copy(
                send_back.at[c, lev * 2 + var], back_ref.at[c, me], out2.at[c], in2.at[c],
                device_id=(lev, var), device_id_type=MESH,
            ).start()
        pltpu.make_async_copy(send_back.at[c, me], back_ref.at[c, me], own_sem.at[c]).start()

    summed = jnp.sum(total[...], axis=0, keepdims=True)
    summed = sum(summed[:, n * LANES : (n + 1) * LANES] for n in range(CHANNELS // LANES))
    cost_ref[me] = summed
    for lev, var in peers:
        pltpu.make_async_remote_copy(
            cost_ref.at[me], cost_ref.at[me], out3, in3, device_id=(lev, var), device_id_type=MESH
        ).start()
    others = pl.ds(0, DEVICES - 1)
    for c in range(CHUNKS):
        pltpu.make_async_copy(send.at[c, others], send.at[c, others], out1.at[c]).wait()
        pltpu.make_async_copy(send_back.at[c, me], back_ref.at[c, me], own_sem.at[c]).wait()
        pltpu.make_async_copy(send_back.at[c, others], send_back.at[c, others], out2.at[c]).wait()
        pltpu.make_async_copy(back_ref.at[c, others], back_ref.at[c, others], in2.at[c]).wait()
    pltpu.make_async_copy(cost_ref.at[others], cost_ref.at[others], out3).wait()
    pltpu.make_async_copy(cost_ref.at[others], cost_ref.at[others], in3).wait()


def adjoint_kernel(
    back_ref, lat_ref, lon_ref, rad_ref, cost_ref,
    grad_ref, rad_out, mean_ref,
    mixed, flip, staged, rad_sem, grad_sem,
):
    rad_copy = pltpu.make_async_copy(rad_ref, rad_out, rad_sem)
    rad_copy.start()

    def leaving(p, j):
        strip = pl.ds(j * LANES, LANES)
        return pltpu.make_async_copy(staged.at[p, j], grad_ref.at[p, :, strip], grad_sem.at[p, j])

    for c in range(CHUNKS):
        widen(back_ref, c, mixed)

    @pl.loop(0, PLANES)
    def _(p):
        for k in range(STEP):
            pieces = [
                mixed[c, pl.ds(k * ROWS + p * NQ + q, 8, stride=STEP * ROWS), :]
                for c in range(CHUNKS)
                for q in range(NQ)
            ]
            flip[0, k] = jnp.concatenate(pieces, axis=1)
        for number in range(PASSES):
            held = flip.at[number % 2]
            sub = lax.broadcasted_iota(jnp.int32, (8, LON), 0)
            first = lat_ref[p, 0] * held[0]
            last = lat_ref[p, STEP - 1] * held[STEP - 1]
            below = jnp.where(sub == 0, 0.0, pltpu.roll(last, 1, 0))
            here = first
            for k in range(STEP):
                if k < STEP - 1:
                    above = lat_ref[p, k + 1] * held[k + 1]
                else:
                    above = jnp.where(sub == 7, 0.0, pltpu.roll(first, 7, 0))
                value = held[k]
                along = lon_ref[p, k] * value
                value = value + (above + below - (here + here)) + (sideways(along) - (along + along))
                below, here = here, above
                if number < PASSES - 1:
                    flip[1 - number % 2, k] = value
                else:
                    for j in range(STRIPS):
                        staged[p, j, pl.ds(k, 8, stride=STEP), :] = value[:, j * LANES : (j + 1) * LANES]
        for j in range(STRIPS):
            leaving(p, j).start()

    mean_ref[0, 0] = jnp.sum(cost_ref[...]) * (0.5 / (LAT * LON * CHANNELS))
    for p in range(PLANES):
        for j in range(STRIPS):
            leaving(p, j).wait()
    rad_copy.wait()


def shards(
    background, field_ids, filter_table, first_weight, first_bias, second_weight, second_bias,
    predictor_index, predictor_coef, channel_level, observed,
):
    vmem = pl.BlockSpec(memory_space=pltpu.VMEM)
    smem = pl.BlockSpec(memory_space=pltpu.SMEM)
    anywhere = pl.BlockSpec(memory_space=pltpu.HBM)
    dma = pltpu.SemaphoreType.DMA
    message = (CHUNKS, DEVICES, ROWS, LANES)
    coefs = jax.ShapeDtypeStruct((PLANES, STEP, 8, LON), F32)
    outcome = pl.pallas_call(
        forward_kernel,
        out_shape=(
            jax.ShapeDtypeStruct(message, BF16),
            coefs,
            coefs,
            jax.ShapeDtypeStruct((LON, CHANNELS), BF16),
            jax.ShapeDtypeStruct((DEVICES, 1, LANES), F32),
        ),
        in_specs=[anywhere] * 11,
        out_specs=[vmem] * 5,
        scratch_shapes=[
            pltpu.VMEM((PLANES, STRIPS, LAT, LANES), F32),
            pltpu.VMEM((STRIPS, LAT, LANES), jnp.int32),
            pltpu.VMEM((2, STEP, 8, LON), F32),
            pltpu.VMEM((CHUNKS, DEVICES * ROWS, LANES), F32),
            pltpu.VMEM(message, BF16),
            pltpu.VMEM(message, BF16),
            pltpu.VMEM(message, BF16),
            pltpu.VMEM((FEATURES, UNITS), BF16),
            pltpu.VMEM((FEATURES, UNITS), BF16),
            pltpu.VMEM((UNITS, CHANNELS), BF16),
            pltpu.VMEM((LON, CHANNELS), F32),
            pltpu.VMEM((FEATURES, CHANNELS), BF16),
            pltpu.VMEM((FEATURES, CHANNELS), BF16),
            pltpu.VMEM((FEATURES, LANES), F32),
            pltpu.VMEM((FEATURES, BLOCK), F32),
            pltpu.SMEM((PLANES, 2, FIELDS), F32),
            pltpu.VMEM((1, UNITS), F32),
            pltpu.VMEM((1, CHANNELS), F32),
            pltpu.VMEM((TERMS, CHANNELS), jnp.int32),
            pltpu.VMEM((TERMS, CHANNELS), F32),
            pltpu.VMEM((1, CHANNELS), jnp.int32),
            pltpu.VMEM((8, CHANNELS), F32),
            dma((PLANES, STRIPS)), dma((STRIPS,)), dma, dma((5,)), dma, dma, dma,
            dma((CHUNKS,)), dma((CHUNKS,)), dma((CHUNKS,)), dma((CHUNKS,)), dma((CHUNKS,)), dma, dma,
        ],
        compiler_params=pltpu.CompilerParams(
            collective_id=0, has_side_effects=True, vmem_limit_bytes=40 * 1024 * 1024
        ),
    )(
        *(
            pltpu.with_memory_space_constraint(operand, pltpu.HBM)
            for operand in (
                background.reshape(PLANES, LAT, LON),
                field_ids,
                filter_table.transpose(1, 2, 3, 0).reshape(PLANES, 2, FIELDS),
                first_weight,
                first_bias.reshape(1, UNITS),
                second_weight,
                second_bias.reshape(1, CHANNELS),
                predictor_index.T,
                predictor_coef.T,
                channel_level.reshape(1, CHANNELS),
                observed.reshape(LON, CHANNELS),
            )
        )
    )
    gradient, radiances, mean_cost = pl.pallas_call(
        adjoint_kernel,
        out_shape=(
            jax.ShapeDtypeStruct((PLANES, LAT, LON), F32),
            jax.ShapeDtypeStruct((LON, CHANNELS), BF16),
            jax.ShapeDtypeStruct((1, 1), F32),
        ),
        in_specs=[vmem] * 5,
        out_specs=[anywhere, anywhere, smem],
        scratch_shapes=[
            pltpu.VMEM((CHUNKS, DEVICES * ROWS, LANES), F32),
            pltpu.VMEM((2, STEP, 8, LON), F32),
            pltpu.VMEM((PLANES, STRIPS, LAT, LANES), F32),
            dma,
            dma((PLANES, STRIPS)),
        ],
        compiler_params=pltpu.CompilerParams(vmem_limit_bytes=24 * 1024 * 1024),
    )(*outcome)
    return (
        radiances.reshape(1, LON, CHANNELS),
        mean_cost.reshape(()),
        gradient.reshape(2, 2, LAT, LON),
    )


def solution(mesh):
    placed = (
        P("lev", "var", None, None), P(), P(None, "lev", "var", None), P(), P(), P(), P(), P(), P(), P(),
        P(("lev", "var"), None, None),
    )
    return jax.shard_map(
        shards,
        mesh=mesh,
        in_specs=placed,
        out_specs=(P(("lev", "var"), None, None), P(), P("lev", "var", None, None)),
        check_vma=False,
    )
```

```python
import functools

import jax
import jax.numpy as jnp
from jax import lax
from jax.experimental import pallas as pl
from jax.experimental.pallas import tpu as pltpu
from jax.sharding import PartitionSpec as P

PASSES = 4
DEVICES = 128
PLANES = 4
FIELDS = 8
TERMS = 8
LAT, LON = 128, 1024
STEP = 16
LANES = 128
STRIPS = 1024 // LANES
NQ = 2
CHUNKS = LON // (LANES * NQ)
ROWS = PLANES * NQ
COLS = LANES * NQ
BLOCK = 256
FEATURES, UNITS, CHANNELS = 512, 1024, 512
MESH = pl.DeviceIdType.MESH
F32, BF16 = jnp.float32, jnp.bfloat16


def offset_of(number):
    return (number // 32, (number // 8) % 4, (number // 2) % 4, number % 2)


def hops_of(number):
    return sum(min(part, 4 - part) for part in offset_of(number)[:3])


ORDER = sorted(range(1, DEVICES), key=lambda n: (-hops_of(n), (n * 73 + 19) * 2654435761 % 4294967291))


def targets():
    lev, var = lax.axis_index("lev"), lax.axis_index("var")
    z, high, y, core = lev // 16, (lev // 8) % 2, (lev // 2) % 4, lev % 2
    x = high * 2 + var
    zs = [((z + d) % 4) * 16 for d in range(4)]
    ys = [((y + d) % 4) * 2 for d in range(4)]
    xs = [(x + d) % 4 for d in range(4)]
    cores = [(core + d) % 2 for d in range(2)]
    zy = [[a + b for b in ys] for a in zs]
    xc = [[(a // 2) * 8 + b for b in cores] for a in xs]
    low = [a % 2 for a in xs]
    found = []
    for number in ORDER:
        dz, dy, dx, dc = offset_of(number)
        found.append((zy[dz][dy] + xc[dx][dc], low[dx]))
    near = [(z * 16 + y * 2 + b + (a // 2) * 8, a % 2) for n, (a, b) in enumerate((a, b) for a in xs for b in cores) if n]
    far = [(c + high * 8 + core, var) for n, c in enumerate(c for row in zy for c in row) if n]
    return lev * 2 + var, found, (x * 2 + core, near), (z * 4 + y, far)


def scatter_rows(where, start, step, values):
    where[pl.ds(start, 8, stride=step), :] = values


def gather_rows(strips, k):
    return jnp.concatenate([strip[pl.ds(k, 8, stride=STEP), :] for strip in strips], axis=1)


def neighbours(held, k):
    sub = lax.broadcasted_iota(jnp.int32, (8, LON), 0)
    if k < STEP - 1:
        above = held[k + 1]
    else:
        above = jnp.where(sub == 7, 0.0, pltpu.roll(held[0], 7, 0))
    if k > 0:
        below = held[k - 1]
    else:
        below = jnp.where(sub == 0, 0.0, pltpu.roll(held[STEP - 1], 1, 0))
    return above, below


def sideways(value):
    return pltpu.roll(value, 1, 1) + pltpu.roll(value, LON - 1, 1)


def coefficient_fields(p, ids, table_ref, lat_ref, lon_ref):
    lane = lax.broadcasted_iota(jnp.int32, (8, LANES), 0)
    for axis, where in ((0, lat_ref), (1, lon_ref)):
        table = jnp.zeros((8, LANES), F32)
        for n in range(FIELDS):
            table = jnp.where(lane == n, table_ref[p, axis, n], table)
        for k in range(STEP):
            for j in range(STRIPS):
                field = ids[j, pl.ds(k, 8, stride=STEP), :]
                where[p, k, :, j * LANES : (j + 1) * LANES] = jnp.take_along_axis(
                    table, field, axis=0, mode="promise_in_bounds"
                )


def smooth(p, planes, flip, lat_ref, lon_ref, mixed):
    for k in range(STEP):
        flip[0, k] = gather_rows([planes.at[p, j] for j in range(STRIPS)], k)
    for number in range(PASSES):
        held = flip.at[number % 2]
        for k in range(STEP):
            above, below = neighbours(held, k)
            value = held[k]
            twice = value + value
            value = (
                value
                + lat_ref[p, k] * (above + below - twice)
                + lon_ref[p, k] * (sideways(value) - twice)
            )
            if number < PASSES - 1:
                flip[1 - number % 2, k] = value
            else:
                for j in range(STRIPS):
                    scatter_rows(mixed.at[p], k * STRIPS + j, STEP * STRIPS, value[:, j * LANES : (j + 1) * LANES])


def narrow(mixed, c, send):
    @pl.loop(0, DEVICES, unroll=4)
    def _(d):
        send[c, d] = mixed[c, pl.ds(pl.multiple_of(d * ROWS, ROWS), ROWS), :].astype(BF16)


def widen(got, c, mixed):
    @pl.loop(0, DEVICES, unroll=4)
    def _(d):
        mixed[c, pl.ds(pl.multiple_of(d * ROWS, ROWS), ROWS), :] = got[c, d].astype(F32)


def selection(index_ref, coef_ref, level_ref, sel):
    @pl.loop(0, FEATURES // 64)
    def _(group):
        row = lax.broadcasted_iota(jnp.int32, (64, CHANNELS), 0)
        feature = row * 8 + (group // 4) * 4 + (group % 2) * 2 + (group // 2) % 2
        picks = jnp.where(feature // 4 == level_ref[...], 1.0, 0.0).astype(F32)
        for n in range(TERMS):
            picks = picks + jnp.where(feature == index_ref[n : n + 1, :], coef_ref[n : n + 1, :], 0.0)
        sel[pl.ds(pl.multiple_of(group * 64, 64), 64), :] = picks.astype(BF16)


def regroup(w1raw, turned, w1):
    for part in range(UNITS // LANES):
        turned[...] = w1raw[:, part * LANES : (part + 1) * LANES].astype(F32)
        for s in range(8):
            block = turned[pl.ds(s, 64, stride=8), :]
            at = ((s // 4) * 2 + s % 2) * LANES + ((s // 2) % 2) * 64
            w1[at : at + 64, part * LANES : (part + 1) * LANES] = block.astype(BF16)


def network(c, arrived, mixed, turned, w1, b1_ref, w2, b2_ref, sel, obs, rad_ref, total):
    for part in range(COLS // BLOCK):
        tiles = range(part * BLOCK // LANES, (part + 1) * BLOCK // LANES)
        for n, q in enumerate(tiles):
            for p in range(PLANES):
                for var in range(2):
                    block = arrived[p, pl.ds(var * STRIPS + c * NQ + q, 64, stride=2 * STRIPS), :]
                    at = p * LANES + var * 64
                    turned[at : at + 64, n * LANES : (n + 1) * LANES] = block
        columns = turned[...].T.astype(BF16)
        spot = pl.ds(pl.multiple_of(c * COLS + part * BLOCK, BLOCK), BLOCK)
        active = jnp.tanh(jnp.dot(columns, w1[...], preferred_element_type=F32) + b1_ref[...])
        evolved = jnp.dot(active.astype(BF16), w2[...], preferred_element_type=F32) + b2_ref[...]
        evolved = evolved + jnp.dot(columns, sel[...], preferred_element_type=F32)
        rad_ref[spot, :] = evolved.astype(BF16)
        depart = evolved - obs[spot, :]
        total[...] += jnp.sum((depart * depart).reshape(BLOCK // 8, 8, CHANNELS), axis=0)
        depart_low = depart.astype(BF16)
        turn = (((1,), (1,)), ((), ()))
        pull = lax.dot_general(depart_low, w2[...], turn, preferred_element_type=F32)
        pull = (pull * (1.0 - active * active)).astype(BF16)
        slope = lax.dot_general(w1[...], pull, turn, preferred_element_type=F32)
        slope = slope + lax.dot_general(sel[...], depart_low, turn, preferred_element_type=F32)
        for n, q in enumerate(tiles):
            for p in range(PLANES):
                for var in range(2):
                    at = p * LANES + var * 64
                    block = slope[at : at + 64, n * LANES : (n + 1) * LANES]
                    mixed[c, pl.ds(var * ROWS + p * NQ + q, 64, stride=2 * ROWS), :] = block


def forward_kernel(
    grid_ref, ids_ref, table_hbm, w1_ref, b1_hbm, w2_ref, b2_hbm, index_hbm, coef_hbm, level_hbm, seen_ref,
    back_ref, lat_ref, lon_ref, rad_ref, cost_ref,
    planes, ids, flip, arrived, mixed, send, got, send_back, back, near_ref, w1raw, w1, w2, obs, sel, strip, turned,
    table_ref, b1_ref, b2_ref, index_ref, coef_ref, level_ref, total,
    grid_sem, ids_sem, table_sem, small_sem, w1_sem, w2_sem, obs_sem, own_sem, out1, in1, out2, in2, out3, in3, out4, in4,
):
    me, peers, (near, near_peers), (far, far_peers) = targets()
    strips = [pl.ds(j * LANES, LANES) for j in range(STRIPS)]
    ids_copies = [pltpu.make_async_copy(ids_ref.at[:, s], ids.at[j], ids_sem.at[j]) for j, s in enumerate(strips)]
    for copy in ids_copies:
        copy.start()
    table_copy = pltpu.make_async_copy(table_hbm, table_ref, table_sem)
    table_copy.start()
    grid_copies = [
        pltpu.make_async_copy(grid_ref.at[p, :, s], planes.at[p, j], grid_sem.at[p, j])
        for p in range(PLANES)
        for j, s in enumerate(strips)
    ]
    for copy in grid_copies:
        copy.start()
    w1_copy = pltpu.make_async_copy(w1_ref, w1raw, w1_sem)
    w2_copy = pltpu.make_async_copy(w2_ref, w2, w2_sem)
    obs_copy = pltpu.make_async_copy(seen_ref, obs, obs_sem)
    small_copies = [
        pltpu.make_async_copy(here, there, small_sem.at[n])
        for n, (here, there) in enumerate(
            (
                (index_hbm, index_ref), (coef_hbm, coef_ref), (level_hbm, level_ref), (b1_hbm, b1_ref), (b2_hbm, b2_ref)
            )
        )
    ]
    for copy in small_copies:
        copy.start()
    w1_copy.start()
    w2_copy.start()
    obs_copy.start()

    barrier = pltpu.get_barrier_semaphore()
    for lev, var in peers:
        pl.semaphore_signal(barrier, 1, device_id=(lev, var), device_id_type=MESH)

    for copy in ids_copies:
        copy.wait()
    table_copy.wait()

    def outward(p):
        def one(lev, var):
            pltpu.make_async_remote_copy(
                send.at[p, lev * 2 + var], got.at[p, me], out1.at[p], in1.at[p],
                device_id=(lev, var), device_id_type=MESH,
            ).start()

        yield from (functools.partial(one, lev, var) for lev, var in peers)
        yield pltpu.make_async_copy(send.at[p, me], got.at[p, me], own_sem.at[p]).start

    def homeward(c):
        def one(lev, var):
            pltpu.make_async_remote_copy(
                send_back.at[c, lev * 2 + var], back.at[c, me], out2.at[c], in2.at[c],
                device_id=(lev, var), device_id_type=MESH,
            ).start()

        yield from (functools.partial(one, lev, var) for lev, var in peers)
        yield pltpu.make_async_copy(send_back.at[c, me], back.at[c, me], own_sem.at[c]).start

    @pl.loop(0, PLANES)
    def _(p):
        coefficient_fields(p, ids, table_ref, lat_ref, lon_ref)
        for j, s in enumerate(strips):
            pltpu.make_async_copy(grid_ref.at[p, :, s], planes.at[p, j], grid_sem.at[p, j]).wait()
        smooth(p, planes, flip, lat_ref, lon_ref, arrived)
        narrow(arrived, p, send)

        @pl.when(p == 0)
        def _():
            pl.semaphore_wait(barrier, DEVICES - 1)

        for start in outward(p):
            start()

    for copy in small_copies:
        copy.wait()
    selection(index_ref, coef_ref, level_ref, sel)
    w1_copy.wait()
    regroup(w1raw, strip, w1)
    w2_copy.wait()
    obs_copy.wait()
    total[...] = jnp.zeros_like(total)
    others = pl.ds(0, DEVICES - 1)

    @pl.loop(0, PLANES)
    def _(p):
        pltpu.make_async_copy(send.at[p, me], got.at[p, me], own_sem.at[p]).wait()
        pltpu.make_async_copy(got.at[p, others], got.at[p, others], in1.at[p]).wait()
        widen(got, p, arrived)

    def chunk(c):
        network(c, arrived, mixed, turned, w1, b1_ref, w2, b2_ref, sel, obs, rad_ref, total)
        narrow(mixed, c, send_back)

    @pl.loop(0, CHUNKS)
    def _(c):
        chunk(c)

        @pl.when(c == CHUNKS - 1)
        def _():
            summed = jnp.sum(total[...], axis=0, keepdims=True)
            near_ref[near] = sum(summed[:, n * LANES : (n + 1) * LANES] for n in range(CHANNELS // LANES))
            for lev, var in near_peers:
                pltpu.make_async_remote_copy(
                    near_ref.at[near], near_ref.at[near], out3, in3, device_id=(lev, var), device_id_type=MESH
                ).start()

        for start in homeward(c):
            start()

    pltpu.make_async_copy(near_ref.at[pl.ds(0, 7)], near_ref.at[pl.ds(0, 7)], out3).wait()
    pltpu.make_async_copy(near_ref.at[pl.ds(0, 7)], near_ref.at[pl.ds(0, 7)], in3).wait()
    cost_ref[far] = jnp.sum(near_ref[...], axis=0)
    for lev, var in far_peers:
        pltpu.make_async_remote_copy(
            cost_ref.at[far], cost_ref.at[far], out4, in4, device_id=(lev, var), device_id_type=MESH
        ).start()
    for c in range(CHUNKS):
        pltpu.make_async_copy(send_back.at[c, me], back.at[c, me], own_sem.at[c]).wait()
        pltpu.make_async_copy(back.at[c, others], back.at[c, others], in2.at[c]).wait()
        widen(back, c, back_ref)
    for c in range(CHUNKS):
        pltpu.make_async_copy(send_back.at[c, others], send_back.at[c, others], out2.at[c]).wait()
    for p in range(PLANES):
        pltpu.make_async_copy(send.at[p, others], send.at[p, others], out1.at[p]).wait()
    pltpu.make_async_copy(cost_ref.at[pl.ds(0, 15)], cost_ref.at[pl.ds(0, 15)], out4).wait()
    pltpu.make_async_copy(cost_ref.at[pl.ds(0, 15)], cost_ref.at[pl.ds(0, 15)], in4).wait()


def unsmooth(p, mixed, flip, lat_ref, lon_ref, staged):
    for k in range(STEP):
        pieces = [
            mixed[c, pl.ds(k * ROWS + p * NQ + q, 8, stride=STEP * ROWS), :]
            for c in range(CHUNKS)
            for q in range(NQ)
        ]
        flip[0, k] = jnp.concatenate(pieces, axis=1)
    for number in range(PASSES):
        held = flip.at[number % 2]
        sub = lax.broadcasted_iota(jnp.int32, (8, LON), 0)
        first = lat_ref[p, 0] * held[0]
        last = lat_ref[p, STEP - 1] * held[STEP - 1]
        below = jnp.where(sub == 0, 0.0, pltpu.roll(last, 1, 0))
        here = first
        for k in range(STEP):
            if k < STEP - 1:
                above = lat_ref[p, k + 1] * held[k + 1]
            else:
                above = jnp.where(sub == 7, 0.0, pltpu.roll(first, 7, 0))
            value = held[k]
            along = lon_ref[p, k] * value
            value = value + (above + below - (here + here)) + (sideways(along) - (along + along))
            below, here = here, above
            if number < PASSES - 1:
                flip[1 - number % 2, k] = value
            else:
                for j in range(STRIPS):
                    staged[p, j, pl.ds(k, 8, stride=STEP), :] = value[:, j * LANES : (j + 1) * LANES]


def unsmooth(p, mixed, flip, lat_ref, lon_ref, staged):
    for k in range(STEP):
        pieces = [
            mixed[c, pl.ds(k * ROWS + p * NQ + q, 8, stride=STEP * ROWS), :]
            for c in range(CHUNKS)
            for q in range(NQ)
        ]
        flip[0, k] = jnp.concatenate(pieces, axis=1)
    for number in range(PASSES):
        held = flip.at[number % 2]
        sub = lax.broadcasted_iota(jnp.int32, (8, LON), 0)
        first = lat_ref[p, 0] * held[0]
        last = lat_ref[p, STEP - 1] * held[STEP - 1]
        below = jnp.where(sub == 0, 0.0, pltpu.roll(last, 1, 0))
        here = first
        for k in range(STEP):
            if k < STEP - 1:
                above = lat_ref[p, k + 1] * held[k + 1]
            else:
                above = jnp.where(sub == 7, 0.0, pltpu.roll(first, 7, 0))
            value = held[k]
            along = lon_ref[p, k] * value
            value = value + (above + below - (here + here)) + (sideways(along) - (along + along))
            below, here = here, above
            if number < PASSES - 1:
                flip[1 - number % 2, k] = value
            else:
                for j in range(STRIPS):
                    staged[p, j, pl.ds(k, 8, stride=STEP), :] = value[:, j * LANES : (j + 1) * LANES]


def adjoint_kernel(
    back_ref, lat_ref, lon_ref, rad_ref, cost_ref,
    grad_ref, rad_out, mean_ref,
    flip, staged, rad_sem, grad_sem,
):
    rad_copy = pltpu.make_async_copy(rad_ref, rad_out, rad_sem)
    rad_copy.start()

    def leaving(p, j):
        strip = pl.ds(j * LANES, LANES)
        return pltpu.make_async_copy(staged.at[p, j], grad_ref.at[p, :, strip], grad_sem.at[p, j])

    @pl.loop(0, PLANES)
    def _(p):
        unsmooth(p, back_ref, flip, lat_ref, lon_ref, staged)
        for j in range(STRIPS):
            leaving(p, j).start()

    mean_ref[0, 0] = jnp.sum(cost_ref[...]) * (0.5 / (LAT * LON * CHANNELS))
    for p in range(PLANES):
        for j in range(STRIPS):
            leaving(p, j).wait()
    rad_copy.wait()


def shards(
    background, field_ids, filter_table, first_weight, first_bias, second_weight, second_bias,
    predictor_index, predictor_coef, channel_level, observed,
):
    vmem = pl.BlockSpec(memory_space=pltpu.VMEM)
    smem = pl.BlockSpec(memory_space=pltpu.SMEM)
    anywhere = pl.BlockSpec(memory_space=pltpu.HBM)
    dma = pltpu.SemaphoreType.DMA
    message = (CHUNKS, DEVICES, ROWS, LANES)
    coefs = jax.ShapeDtypeStruct((PLANES, STEP, 8, LON), F32)
    outcome = pl.pallas_call(
        forward_kernel,
        out_shape=(
            jax.ShapeDtypeStruct((CHUNKS, DEVICES * ROWS, LANES), F32),
            coefs,
            coefs,
            jax.ShapeDtypeStruct((LON, CHANNELS), BF16),
            jax.ShapeDtypeStruct((DEVICES // 8, 1, LANES), F32),
        ),
        in_specs=[anywhere] * 11,
        out_specs=[vmem] * 5,
        scratch_shapes=[
            pltpu.VMEM((PLANES, STRIPS, LAT, LANES), F32),
            pltpu.VMEM((STRIPS, LAT, LANES), jnp.int32),
            pltpu.VMEM((2, STEP, 8, LON), F32),
            pltpu.VMEM((PLANES, DEVICES * STRIPS, LANES), F32),
            pltpu.VMEM((CHUNKS, DEVICES * ROWS, LANES), F32),
            pltpu.VMEM((PLANES, DEVICES, STRIPS, LANES), BF16),
            pltpu.VMEM((PLANES, DEVICES, STRIPS, LANES), BF16),
            pltpu.VMEM(message, BF16),
            pltpu.VMEM(message, BF16),
            pltpu.VMEM((8, 1, LANES), F32),
            pltpu.VMEM((FEATURES, UNITS), BF16),
            pltpu.VMEM((FEATURES, UNITS), BF16),
            pltpu.VMEM((UNITS, CHANNELS), BF16),
            pltpu.VMEM((LON, CHANNELS), F32),
            pltpu.VMEM((FEATURES, CHANNELS), BF16),
            pltpu.VMEM((FEATURES, LANES), F32),
            pltpu.VMEM((FEATURES, BLOCK), F32),
            pltpu.SMEM((PLANES, 2, FIELDS), F32),
            pltpu.VMEM((1, UNITS), F32),
            pltpu.VMEM((1, CHANNELS), F32),
            pltpu.VMEM((TERMS, CHANNELS), jnp.int32),
            pltpu.VMEM((TERMS, CHANNELS), F32),
            pltpu.VMEM((1, CHANNELS), jnp.int32),
            pltpu.VMEM((8, CHANNELS), F32),
            dma((PLANES, STRIPS)), dma((STRIPS,)), dma, dma((5,)), dma, dma, dma,
            dma((PLANES,)), dma((PLANES,)), dma((PLANES,)), dma((CHUNKS,)), dma((CHUNKS,)), dma, dma, dma, dma,
        ],
        compiler_params=pltpu.CompilerParams(
            collective_id=0, has_side_effects=True, vmem_limit_bytes=40 * 1024 * 1024
        ),
    )(
        *(
            pltpu.with_memory_space_constraint(operand, pltpu.HBM)
            for operand in (
                background.reshape(PLANES, LAT, LON),
                field_ids,
                filter_table.transpose(1, 2, 3, 0).reshape(PLANES, 2, FIELDS),
                first_weight,
                first_bias.reshape(1, UNITS),
                second_weight,
                second_bias.reshape(1, CHANNELS),
                predictor_index.T,
                predictor_coef.T,
                channel_level.reshape(1, CHANNELS),
                observed.reshape(LON, CHANNELS),
            )
        )
    )
    gradient, radiances, mean_cost = pl.pallas_call(
        adjoint_kernel,
        out_shape=(
            jax.ShapeDtypeStruct((PLANES, LAT, LON), F32),
            jax.ShapeDtypeStruct((LON, CHANNELS), BF16),
            jax.ShapeDtypeStruct((1, 1), F32),
        ),
        in_specs=[vmem] * 5,
        out_specs=[anywhere, anywhere, smem],
        scratch_shapes=[
            pltpu.VMEM((2, STEP, 8, LON), F32),
            pltpu.VMEM((PLANES, STRIPS, LAT, LANES), F32),
            dma,
            dma((PLANES, STRIPS)),
        ],
        compiler_params=pltpu.CompilerParams(vmem_limit_bytes=24 * 1024 * 1024),
    )(*outcome)
    return (
        radiances.reshape(1, LON, CHANNELS),
        mean_cost.reshape(()),
        gradient.reshape(2, 2, LAT, LON),
    )


def solution(mesh):
    placed = (
        P("lev", "var", None, None), P(), P(None, "lev", "var", None), P(), P(), P(), P(), P(), P(), P(),
        P(("lev", "var"), None, None),
    )
    return jax.shard_map(
        shards,
        mesh=mesh,
        in_specs=placed,
        out_specs=(P(("lev", "var"), None, None), P(), P("lev", "var", None, None)),
        check_vma=False,
    )
```

```python
import functools

import jax
import jax.numpy as jnp
from jax import lax
from jax.experimental import pallas as pl
from jax.experimental.pallas import tpu as pltpu
from jax.sharding import PartitionSpec as P

PASSES = 4
DEVICES = 128
PLANES = 4
FIELDS = 8
TERMS = 8
LAT, LON = 128, 1024
STEP = 16
LANES = 128
STRIPS = 1024 // LANES
NQ = 2
CHUNKS = LON // (LANES * NQ)
ROWS = PLANES * NQ
COLS = LANES * NQ
BLOCK = 256
FEATURES, UNITS, CHANNELS = 512, 1024, 512
MESH = pl.DeviceIdType.MESH
F32, BF16 = jnp.float32, jnp.bfloat16


def offset_of(number):
    return (number // 32, (number // 8) % 4, (number // 2) % 4, number % 2)


def hops_of(number):
    return sum(min(part, 4 - part) for part in offset_of(number)[:3])


ORDER = sorted(range(1, DEVICES), key=lambda n: (-hops_of(n), (n * 73 + 19) * 2654435761 % 4294967291))


def targets():
    lev, var = lax.axis_index("lev"), lax.axis_index("var")
    z, high, y, core = lev // 16, (lev // 8) % 2, (lev // 2) % 4, lev % 2
    x = high * 2 + var
    zs = [((z + d) % 4) * 16 for d in range(4)]
    ys = [((y + d) % 4) * 2 for d in range(4)]
    xs = [(x + d) % 4 for d in range(4)]
    cores = [(core + d) % 2 for d in range(2)]
    zy = [[a + b for b in ys] for a in zs]
    xc = [[(a // 2) * 8 + b for b in cores] for a in xs]
    low = [a % 2 for a in xs]
    found = []
    for number in ORDER:
        dz, dy, dx, dc = offset_of(number)
        found.append((zy[dz][dy] + xc[dx][dc], low[dx]))
    near = [(z * 16 + y * 2 + b + (a // 2) * 8, a % 2) for n, (a, b) in enumerate((a, b) for a in xs for b in cores) if n]
    far = [(c + high * 8 + core, var) for n, c in enumerate(c for row in zy for c in row) if n]
    return lev * 2 + var, found, (x * 2 + core, near), (z * 4 + y, far)


def scatter_rows(where, start, step, values):
    where[pl.ds(start, 8, stride=step), :] = values


def gather_rows(strips, k):
    return jnp.concatenate([strip[pl.ds(k, 8, stride=STEP), :] for strip in strips], axis=1)


def neighbours(held, k):
    sub = lax.broadcasted_iota(jnp.int32, (8, LON), 0)
    if k < STEP - 1:
        above = held[k + 1]
    else:
        above = jnp.where(sub == 7, 0.0, pltpu.roll(held[0], 7, 0))
    if k > 0:
        below = held[k - 1]
    else:
        below = jnp.where(sub == 0, 0.0, pltpu.roll(held[STEP - 1], 1, 0))
    return above, below


def sideways(value):
    return pltpu.roll(value, 1, 1) + pltpu.roll(value, LON - 1, 1)


def coefficient_fields(p, ids, table_ref, lat_ref, lon_ref):
    lane = lax.broadcasted_iota(jnp.int32, (8, LANES), 0)
    for axis, where in ((0, lat_ref), (1, lon_ref)):
        table = jnp.zeros((8, LANES), F32)
        for n in range(FIELDS):
            table = jnp.where(lane == n, table_ref[p, axis, n], table)
        for k in range(STEP):
            for j in range(STRIPS):
                field = ids[j, pl.ds(k, 8, stride=STEP), :]
                where[p, k, :, j * LANES : (j + 1) * LANES] = jnp.take_along_axis(
                    table, field, axis=0, mode="promise_in_bounds"
                )


def smooth(p, planes, flip, lat_ref, lon_ref, mixed):
    for k in range(STEP):
        flip[0, k] = gather_rows([planes.at[p, j] for j in range(STRIPS)], k)
    for number in range(PASSES):
        held = flip.at[number % 2]
        for k in range(STEP):
            above, below = neighbours(held, k)
            value = held[k]
            twice = value + value
            value = (
                value
                + lat_ref[p, k] * (above + below - twice)
                + lon_ref[p, k] * (sideways(value) - twice)
            )
            if number < PASSES - 1:
                flip[1 - number % 2, k] = value
            else:
                for j in range(STRIPS):
                    scatter_rows(mixed.at[p], k * STRIPS + j, STEP * STRIPS, value[:, j * LANES : (j + 1) * LANES])


def narrow(mixed, c, send):
    @pl.loop(0, DEVICES, unroll=16)
    def _(d):
        send[c, d] = mixed[c, pl.ds(pl.multiple_of(d * ROWS, ROWS), ROWS), :].astype(BF16)


def widen(got, c, mixed):
    @pl.loop(0, DEVICES, unroll=16)
    def _(d):
        mixed[c, pl.ds(pl.multiple_of(d * ROWS, ROWS), ROWS), :] = got[c, d].astype(F32)


def selection(index_ref, coef_ref, level_ref, sel):
    @pl.loop(0, FEATURES // 64)
    def _(group):
        row = lax.broadcasted_iota(jnp.int32, (64, CHANNELS), 0)
        feature = row * 8 + (group // 4) * 4 + (group % 2) * 2 + (group // 2) % 2
        picks = jnp.where(feature // 4 == level_ref[...], 1.0, 0.0).astype(F32)
        for n in range(TERMS):
            picks = picks + jnp.where(feature == index_ref[n : n + 1, :], coef_ref[n : n + 1, :], 0.0)
        sel[pl.ds(pl.multiple_of(group * 64, 64), 64), :] = picks.astype(BF16)


def regroup(w1raw, turned, w1):
    for part in range(UNITS // LANES):
        turned[...] = w1raw[:, part * LANES : (part + 1) * LANES].astype(F32)
        for s in range(8):
            block = turned[pl.ds(s, 64, stride=8), :]
            at = ((s // 4) * 2 + s % 2) * LANES + ((s // 2) % 2) * 64
            w1[at : at + 64, part * LANES : (part + 1) * LANES] = block.astype(BF16)


def network(c, arrived, mixed, turned, w1, b1_ref, w2, b2_ref, sel, obs, rad_ref, total):
    for part in range(COLS // BLOCK):
        tiles = range(part * BLOCK // LANES, (part + 1) * BLOCK // LANES)
        for n, q in enumerate(tiles):
            for p in range(PLANES):
                for var in range(2):
                    block = arrived[p, pl.ds(var * STRIPS + c * NQ + q, 64, stride=2 * STRIPS), :]
                    at = p * LANES + var * 64
                    turned[at : at + 64, n * LANES : (n + 1) * LANES] = block
        columns = turned[...].T.astype(BF16)
        spot = pl.ds(pl.multiple_of(c * COLS + part * BLOCK, BLOCK), BLOCK)
        active = jnp.tanh(jnp.dot(columns, w1[...], preferred_element_type=F32) + b1_ref[...])
        evolved = jnp.dot(active.astype(BF16), w2[...], preferred_element_type=F32) + b2_ref[...]
        evolved = evolved + jnp.dot(columns, sel[...], preferred_element_type=F32)
        rad_ref[spot, :] = evolved.astype(BF16)
        depart = evolved - obs[spot, :]
        total[...] += jnp.sum((depart * depart).reshape(BLOCK // 8, 8, CHANNELS), axis=0)
        depart_low = depart.astype(BF16)
        turn = (((1,), (1,)), ((), ()))
        pull = lax.dot_general(depart_low, w2[...], turn, preferred_element_type=F32)
        pull = (pull * (1.0 - active * active)).astype(BF16)
        slope = lax.dot_general(w1[...], pull, turn, preferred_element_type=F32)
        slope = slope + lax.dot_general(sel[...], depart_low, turn, preferred_element_type=F32)
        for n, q in enumerate(tiles):
            for p in range(PLANES):
                for var in range(2):
                    at = p * LANES + var * 64
                    block = slope[at : at + 64, n * LANES : (n + 1) * LANES]
                    mixed[c, pl.ds(var * ROWS + p * NQ + q, 64, stride=2 * ROWS), :] = block


def forward_kernel(
    grid_ref, ids_ref, table_hbm, w1_ref, b1_hbm, w2_ref, b2_hbm, index_hbm, coef_hbm, level_hbm, seen_ref,
    back_ref, lat_ref, lon_ref, rad_ref, cost_ref,
    planes, ids, flip, arrived, mixed, send, got, send_back, back, near_ref, w1raw, w1, w2, obs, sel, strip, turned,
    table_ref, b1_ref, b2_ref, index_ref, coef_ref, level_ref, total,
    grid_sem, ids_sem, table_sem, small_sem, w1_sem, w2_sem, obs_sem, own_sem, out1, in1, out2, in2, out3, in3, out4, in4,
):
    me, peers, (near, near_peers), (far, far_peers) = targets()
    strips = [pl.ds(j * LANES, LANES) for j in range(STRIPS)]
    ids_copies = [pltpu.make_async_copy(ids_ref.at[:, s], ids.at[j], ids_sem.at[j]) for j, s in enumerate(strips)]
    for copy in ids_copies:
        copy.start()
    table_copy = pltpu.make_async_copy(table_hbm, table_ref, table_sem)
    table_copy.start()
    grid_copies = [
        pltpu.make_async_copy(grid_ref.at[p, :, s], planes.at[p, j], grid_sem.at[p, j])
        for p in range(PLANES)
        for j, s in enumerate(strips)
    ]
    for copy in grid_copies:
        copy.start()
    w1_copy = pltpu.make_async_copy(w1_ref, w1raw, w1_sem)
    w2_copy = pltpu.make_async_copy(w2_ref, w2, w2_sem)
    obs_copy = pltpu.make_async_copy(seen_ref, obs, obs_sem)
    small_copies = [
        pltpu.make_async_copy(here, there, small_sem.at[n])
        for n, (here, there) in enumerate(
            (
                (index_hbm, index_ref), (coef_hbm, coef_ref), (level_hbm, level_ref), (b1_hbm, b1_ref), (b2_hbm, b2_ref)
            )
        )
    ]
    for copy in small_copies:
        copy.start()
    w1_copy.start()
    w2_copy.start()
    obs_copy.start()

    barrier = pltpu.get_barrier_semaphore()
    for lev, var in peers:
        pl.semaphore_signal(barrier, 1, device_id=(lev, var), device_id_type=MESH)

    for copy in ids_copies:
        copy.wait()
    table_copy.wait()

    def outward(p):
        def one(lev, var):
            pltpu.make_async_remote_copy(
                send.at[p, lev * 2 + var], got.at[p, me], out1.at[p], in1.at[p],
                device_id=(lev, var), device_id_type=MESH,
            ).start()

        yield from (functools.partial(one, lev, var) for lev, var in peers)
        yield pltpu.make_async_copy(send.at[p, me], got.at[p, me], own_sem.at[p]).start

    def homeward(c):
        def one(lev, var):
            pltpu.make_async_remote_copy(
                send_back.at[c, lev * 2 + var], back.at[c, me], out2.at[c], in2.at[c],
                device_id=(lev, var), device_id_type=MESH,
            ).start()

        yield from (functools.partial(one, lev, var) for lev, var in peers)
        yield pltpu.make_async_copy(send_back.at[c, me], back.at[c, me], own_sem.at[c]).start

    @pl.loop(0, PLANES)
    def _(p):
        coefficient_fields(p, ids, table_ref, lat_ref, lon_ref)
        for j, s in enumerate(strips):
            pltpu.make_async_copy(grid_ref.at[p, :, s], planes.at[p, j], grid_sem.at[p, j]).wait()
        smooth(p, planes, flip, lat_ref, lon_ref, arrived)
        narrow(arrived, p, send)

        @pl.when(p == 0)
        def _():
            pl.semaphore_wait(barrier, DEVICES - 1)

        for start in outward(p):
            start()

    for copy in small_copies:
        copy.wait()
    selection(index_ref, coef_ref, level_ref, sel)
    w1_copy.wait()
    regroup(w1raw, strip, w1)
    w2_copy.wait()
    obs_copy.wait()
    total[...] = jnp.zeros_like(total)
    others = pl.ds(0, DEVICES - 1)

    @pl.loop(0, PLANES)
    def _(p):
        pltpu.make_async_copy(send.at[p, me], got.at[p, me], own_sem.at[p]).wait()
        pltpu.make_async_copy(got.at[p, others], got.at[p, others], in1.at[p]).wait()
        widen(got, p, arrived)

    def chunk(c):
        network(c, arrived, mixed, turned, w1, b1_ref, w2, b2_ref, sel, obs, rad_ref, total)
        narrow(mixed, c, send_back)

    @pl.loop(0, CHUNKS)
    def _(c):
        chunk(c)

        @pl.when(c == CHUNKS - 1)
        def _():
            summed = jnp.sum(total[...], axis=0, keepdims=True)
            near_ref[near] = sum(summed[:, n * LANES : (n + 1) * LANES] for n in range(CHANNELS // LANES))
            for lev, var in near_peers:
                pltpu.make_async_remote_copy(
                    near_ref.at[near], near_ref.at[near], out3, in3, device_id=(lev, var), device_id_type=MESH
                ).start()

        for start in homeward(c):
            start()

    pltpu.make_async_copy(near_ref.at[pl.ds(0, 7)], near_ref.at[pl.ds(0, 7)], out3).wait()
    pltpu.make_async_copy(near_ref.at[pl.ds(0, 7)], near_ref.at[pl.ds(0, 7)], in3).wait()
    cost_ref[far] = jnp.sum(near_ref[...], axis=0)
    for lev, var in far_peers:
        pltpu.make_async_remote_copy(
            cost_ref.at[far], cost_ref.at[far], out4, in4, device_id=(lev, var), device_id_type=MESH
        ).start()
    for c in range(CHUNKS):
        pltpu.make_async_copy(send_back.at[c, me], back.at[c, me], own_sem.at[c]).wait()
        pltpu.make_async_copy(back.at[c, others], back.at[c, others], in2.at[c]).wait()
        widen(back, c, back_ref)
    for c in range(CHUNKS):
        pltpu.make_async_copy(send_back.at[c, others], send_back.at[c, others], out2.at[c]).wait()
    for p in range(PLANES):
        pltpu.make_async_copy(send.at[p, others], send.at[p, others], out1.at[p]).wait()
    pltpu.make_async_copy(cost_ref.at[pl.ds(0, 15)], cost_ref.at[pl.ds(0, 15)], out4).wait()
    pltpu.make_async_copy(cost_ref.at[pl.ds(0, 15)], cost_ref.at[pl.ds(0, 15)], in4).wait()


def unsmooth(p, mixed, flip, lat_ref, lon_ref, staged):
    for k in range(STEP):
        pieces = [
            mixed[c, pl.ds(k * ROWS + p * NQ + q, 8, stride=STEP * ROWS), :]
            for c in range(CHUNKS)
            for q in range(NQ)
        ]
        flip[0, k] = jnp.concatenate(pieces, axis=1)
    for number in range(PASSES):
        held = flip.at[number % 2]
        sub = lax.broadcasted_iota(jnp.int32, (8, LON), 0)
        first = lat_ref[p, 0] * held[0]
        last = lat_ref[p, STEP - 1] * held[STEP - 1]
        below = jnp.where(sub == 0, 0.0, pltpu.roll(last, 1, 0))
        here = first
        for k in range(STEP):
            if k < STEP - 1:
                above = lat_ref[p, k + 1] * held[k + 1]
            else:
                above = jnp.where(sub == 7, 0.0, pltpu.roll(first, 7, 0))
            value = held[k]
            along = lon_ref[p, k] * value
            value = value + (above + below - (here + here)) + (sideways(along) - (along + along))
            below, here = here, above
            if number < PASSES - 1:
                flip[1 - number % 2, k] = value
            else:
                for j in range(STRIPS):
                    staged[p, j, pl.ds(k, 8, stride=STEP), :] = value[:, j * LANES : (j + 1) * LANES]


def unsmooth(p, mixed, flip, lat_ref, lon_ref, staged):
    for k in range(STEP):
        pieces = [
            mixed[c, pl.ds(k * ROWS + p * NQ + q, 8, stride=STEP * ROWS), :]
            for c in range(CHUNKS)
            for q in range(NQ)
        ]
        flip[0, k] = jnp.concatenate(pieces, axis=1)
    for number in range(PASSES):
        held = flip.at[number % 2]
        sub = lax.broadcasted_iota(jnp.int32, (8, LON), 0)
        first = lat_ref[p, 0] * held[0]
        last = lat_ref[p, STEP - 1] * held[STEP - 1]
        below = jnp.where(sub == 0, 0.0, pltpu.roll(last, 1, 0))
        here = first
        for k in range(STEP):
            if k < STEP - 1:
                above = lat_ref[p, k + 1] * held[k + 1]
            else:
                above = jnp.where(sub == 7, 0.0, pltpu.roll(first, 7, 0))
            value = held[k]
            along = lon_ref[p, k] * value
            value = value + (above + below - (here + here)) + (sideways(along) - (along + along))
            below, here = here, above
            if number < PASSES - 1:
                flip[1 - number % 2, k] = value
            else:
                for j in range(STRIPS):
                    staged[p, j, pl.ds(k, 8, stride=STEP), :] = value[:, j * LANES : (j + 1) * LANES]


def adjoint_kernel(
    back_ref, lat_ref, lon_ref, rad_ref, cost_ref,
    grad_ref, rad_out, mean_ref,
    flip, staged, rad_sem, grad_sem,
):
    rad_copy = pltpu.make_async_copy(rad_ref, rad_out, rad_sem)
    rad_copy.start()

    def leaving(p, j):
        strip = pl.ds(j * LANES, LANES)
        return pltpu.make_async_copy(staged.at[p, j], grad_ref.at[p, :, strip], grad_sem.at[p, j])

    @pl.loop(0, PLANES)
    def _(p):
        unsmooth(p, back_ref, flip, lat_ref, lon_ref, staged)
        for j in range(STRIPS):
            leaving(p, j).start()

    mean_ref[0, 0] = jnp.sum(cost_ref[...]) * (0.5 / (LAT * LON * CHANNELS))
    for p in range(PLANES):
        for j in range(STRIPS):
            leaving(p, j).wait()
    rad_copy.wait()


def shards(
    background, field_ids, filter_table, first_weight, first_bias, second_weight, second_bias,
    predictor_index, predictor_coef, channel_level, observed,
):
    vmem = pl.BlockSpec(memory_space=pltpu.VMEM)
    smem = pl.BlockSpec(memory_space=pltpu.SMEM)
    anywhere = pl.BlockSpec(memory_space=pltpu.HBM)
    dma = pltpu.SemaphoreType.DMA
    message = (CHUNKS, DEVICES, ROWS, LANES)
    coefs = jax.ShapeDtypeStruct((PLANES, STEP, 8, LON), F32)
    outcome = pl.pallas_call(
        forward_kernel,
        out_shape=(
            jax.ShapeDtypeStruct((CHUNKS, DEVICES * ROWS, LANES), F32),
            coefs,
            coefs,
            jax.ShapeDtypeStruct((LON, CHANNELS), BF16),
            jax.ShapeDtypeStruct((DEVICES // 8, 1, LANES), F32),
        ),
        in_specs=[anywhere] * 11,
        out_specs=[vmem] * 5,
        scratch_shapes=[
            pltpu.VMEM((PLANES, STRIPS, LAT, LANES), F32),
            pltpu.VMEM((STRIPS, LAT, LANES), jnp.int32),
            pltpu.VMEM((2, STEP, 8, LON), F32),
            pltpu.VMEM((PLANES, DEVICES * STRIPS, LANES), F32),
            pltpu.VMEM((CHUNKS, DEVICES * ROWS, LANES), F32),
            pltpu.VMEM((PLANES, DEVICES, STRIPS, LANES), BF16),
            pltpu.VMEM((PLANES, DEVICES, STRIPS, LANES), BF16),
            pltpu.VMEM(message, BF16),
            pltpu.VMEM(message, BF16),
            pltpu.VMEM((8, 1, LANES), F32),
            pltpu.VMEM((FEATURES, UNITS), BF16),
            pltpu.VMEM((FEATURES, UNITS), BF16),
            pltpu.VMEM((UNITS, CHANNELS), BF16),
            pltpu.VMEM((LON, CHANNELS), F32),
            pltpu.VMEM((FEATURES, CHANNELS), BF16),
            pltpu.VMEM((FEATURES, LANES), F32),
            pltpu.VMEM((FEATURES, BLOCK), F32),
            pltpu.SMEM((PLANES, 2, FIELDS), F32),
            pltpu.VMEM((1, UNITS), F32),
            pltpu.VMEM((1, CHANNELS), F32),
            pltpu.VMEM((TERMS, CHANNELS), jnp.int32),
            pltpu.VMEM((TERMS, CHANNELS), F32),
            pltpu.VMEM((1, CHANNELS), jnp.int32),
            pltpu.VMEM((8, CHANNELS), F32),
            dma((PLANES, STRIPS)), dma((STRIPS,)), dma, dma((5,)), dma, dma, dma,
            dma((PLANES,)), dma((PLANES,)), dma((PLANES,)), dma((CHUNKS,)), dma((CHUNKS,)), dma, dma, dma, dma,
        ],
        compiler_params=pltpu.CompilerParams(
            collective_id=0, has_side_effects=True, vmem_limit_bytes=40 * 1024 * 1024
        ),
    )(
        *(
            pltpu.with_memory_space_constraint(operand, pltpu.HBM)
            for operand in (
                background.reshape(PLANES, LAT, LON),
                field_ids,
                filter_table.transpose(1, 2, 3, 0).reshape(PLANES, 2, FIELDS),
                first_weight,
                first_bias.reshape(1, UNITS),
                second_weight,
                second_bias.reshape(1, CHANNELS),
                predictor_index.T,
                predictor_coef.T,
                channel_level.reshape(1, CHANNELS),
                observed.reshape(LON, CHANNELS),
            )
        )
    )
    gradient, radiances, mean_cost = pl.pallas_call(
        adjoint_kernel,
        out_shape=(
            jax.ShapeDtypeStruct((PLANES, LAT, LON), F32),
            jax.ShapeDtypeStruct((LON, CHANNELS), BF16),
            jax.ShapeDtypeStruct((1, 1), F32),
        ),
        in_specs=[vmem] * 5,
        out_specs=[anywhere, anywhere, smem],
        scratch_shapes=[
            pltpu.VMEM((2, STEP, 8, LON), F32),
            pltpu.VMEM((PLANES, STRIPS, LAT, LANES), F32),
            dma,
            dma((PLANES, STRIPS)),
        ],
        compiler_params=pltpu.CompilerParams(vmem_limit_bytes=24 * 1024 * 1024),
    )(*outcome)
    return (
        radiances.reshape(1, LON, CHANNELS),
        mean_cost.reshape(()),
        gradient.reshape(2, 2, LAT, LON),
    )


def solution(mesh):
    placed = (
        P("lev", "var", None, None), P(), P(None, "lev", "var", None), P(), P(), P(), P(), P(), P(), P(),
        P(("lev", "var"), None, None),
    )
    return jax.shard_map(
        shards,
        mesh=mesh,
        in_specs=placed,
        out_specs=(P(("lev", "var"), None, None), P(), P("lev", "var", None, None)),
        check_vma=False,
    )
```

```python
import functools

import jax
import jax.numpy as jnp
from jax import lax
from jax.experimental import pallas as pl
from jax.experimental.pallas import tpu as pltpu
from jax.sharding import PartitionSpec as P

PASSES = 4
DEVICES = 128
PLANES = 4
FIELDS = 8
TERMS = 8
LAT, LON = 128, 1024
STEP = 16
LANES = 128
STRIPS = 1024 // LANES
NQ = 2
CHUNKS = LON // (LANES * NQ)
ROWS = PLANES * NQ
COLS = LANES * NQ
BLOCK = 256
FEATURES, UNITS, CHANNELS = 512, 1024, 512
MESH = pl.DeviceIdType.MESH
F32, BF16 = jnp.float32, jnp.bfloat16


def offset_of(number):
    return (number // 32, (number // 8) % 4, (number // 2) % 4, number % 2)


def hops_of(number):
    return sum(min(part, 4 - part) for part in offset_of(number)[:3])


ORDER = sorted(range(1, DEVICES), key=lambda n: (-hops_of(n), (n * 73 + 19) * 2654435761 % 4294967291))


def targets():
    lev, var = lax.axis_index("lev"), lax.axis_index("var")
    z, high, y, core = lev // 16, (lev // 8) % 2, (lev // 2) % 4, lev % 2
    x = high * 2 + var
    zs = [((z + d) % 4) * 16 for d in range(4)]
    ys = [((y + d) % 4) * 2 for d in range(4)]
    xs = [(x + d) % 4 for d in range(4)]
    cores = [(core + d) % 2 for d in range(2)]
    zy = [[a + b for b in ys] for a in zs]
    xc = [[(a // 2) * 8 + b for b in cores] for a in xs]
    low = [a % 2 for a in xs]
    found = []
    for number in ORDER:
        dz, dy, dx, dc = offset_of(number)
        found.append((zy[dz][dy] + xc[dx][dc], low[dx]))
    near = [(z * 16 + y * 2 + b + (a // 2) * 8, a % 2) for n, (a, b) in enumerate((a, b) for a in xs for b in cores) if n]
    far = [(c + high * 8 + core, var) for n, c in enumerate(c for row in zy for c in row) if n]
    return lev * 2 + var, found, (x * 2 + core, near), (z * 4 + y, far)


def scatter_rows(where, start, step, values):
    where[pl.ds(start, 8, stride=step), :] = values


def gather_rows(strips, k):
    return jnp.concatenate([strip[pl.ds(k, 8, stride=STEP), :] for strip in strips], axis=1)


def neighbours(held, k):
    sub = lax.broadcasted_iota(jnp.int32, (8, LON), 0)
    if k < STEP - 1:
        above = held[k + 1]
    else:
        above = jnp.where(sub == 7, 0.0, pltpu.roll(held[0], 7, 0))
    if k > 0:
        below = held[k - 1]
    else:
        below = jnp.where(sub == 0, 0.0, pltpu.roll(held[STEP - 1], 1, 0))
    return above, below


def sideways(value):
    return pltpu.roll(value, 1, 1) + pltpu.roll(value, LON - 1, 1)


def coefficients(field, levels):
    bits = [(field & (1 << n)) != 0 for n in range(3)]
    chosen = []
    for level in levels:
        for bit in bits:
            level = [jnp.where(bit, level[2 * n + 1], level[2 * n]) for n in range(len(level) // 2)]
        chosen.append(level[0])
    return chosen


def smooth(p, ids, table_ref, planes, flip, lat_ref, lon_ref, mixed):
    levels = [[table_ref[p, axis, n] for n in range(FIELDS)] for axis in range(2)]
    for k in range(STEP):
        flip[0, k] = gather_rows([planes.at[p, j] for j in range(STRIPS)], k)
    for number in range(PASSES):
        held = flip.at[number % 2]
        for k in range(STEP):
            if number == 0:
                field = gather_rows([ids.at[j] for j in range(STRIPS)], k)
                lat_coef, lon_coef = coefficients(field, levels)
                lat_ref[p, k], lon_ref[p, k] = lat_coef, lon_coef
            else:
                lat_coef, lon_coef = lat_ref[p, k], lon_ref[p, k]
            above, below = neighbours(held, k)
            value = held[k]
            twice = value + value
            value = value + lat_coef * (above + below - twice) + lon_coef * (sideways(value) - twice)
            if number < PASSES - 1:
                flip[1 - number % 2, k] = value
            else:
                for j in range(STRIPS):
                    scatter_rows(mixed.at[p], k * STRIPS + j, STEP * STRIPS, value[:, j * LANES : (j + 1) * LANES])


def narrow(mixed, c, send):
    @pl.loop(0, DEVICES, unroll=16)
    def _(d):
        send[c, d] = mixed[c, pl.ds(pl.multiple_of(d * ROWS, ROWS), ROWS), :].astype(BF16)


def widen(got, c, mixed):
    @pl.loop(0, DEVICES, unroll=16)
    def _(d):
        mixed[c, pl.ds(pl.multiple_of(d * ROWS, ROWS), ROWS), :] = got[c, d].astype(F32)


def selection(index_ref, coef_ref, level_ref, sel):
    @pl.loop(0, FEATURES // 64)
    def _(group):
        row = lax.broadcasted_iota(jnp.int32, (64, CHANNELS), 0)
        feature = row * 8 + (group // 4) * 4 + (group % 2) * 2 + (group // 2) % 2
        picks = jnp.where(feature // 4 == level_ref[...], 1.0, 0.0).astype(F32)
        for n in range(TERMS):
            picks = picks + jnp.where(feature == index_ref[n : n + 1, :], coef_ref[n : n + 1, :], 0.0)
        sel[pl.ds(pl.multiple_of(group * 64, 64), 64), :] = picks.astype(BF16)


def regroup(w1raw, turned, w1):
    for part in range(UNITS // LANES):
        turned[...] = w1raw[:, part * LANES : (part + 1) * LANES].astype(F32)
        for s in range(8):
            block = turned[pl.ds(s, 64, stride=8), :]
            at = ((s // 4) * 2 + s % 2) * LANES + ((s // 2) % 2) * 64
            w1[at : at + 64, part * LANES : (part + 1) * LANES] = block.astype(BF16)


def network(c, arrived, mixed, turned, w1, b1_ref, w2, b2_ref, sel, obs, rad_ref, total):
    for part in range(COLS // BLOCK):
        tiles = range(part * BLOCK // LANES, (part + 1) * BLOCK // LANES)
        for n, q in enumerate(tiles):
            for p in range(PLANES):
                for var in range(2):
                    block = arrived[p, pl.ds(var * STRIPS + c * NQ + q, 64, stride=2 * STRIPS), :]
                    at = p * LANES + var * 64
                    turned[at : at + 64, n * LANES : (n + 1) * LANES] = block
        columns = turned[...].T.astype(BF16)
        spot = pl.ds(pl.multiple_of(c * COLS + part * BLOCK, BLOCK), BLOCK)
        active = jnp.tanh(jnp.dot(columns, w1[...], preferred_element_type=F32) + b1_ref[...])
        evolved = jnp.dot(active.astype(BF16), w2[...], preferred_element_type=F32) + b2_ref[...]
        evolved = evolved + jnp.dot(columns, sel[...], preferred_element_type=F32)
        rad_ref[spot, :] = evolved.astype(BF16)
        depart = evolved - obs[spot, :]
        total[...] += jnp.sum((depart * depart).reshape(BLOCK // 8, 8, CHANNELS), axis=0)
        depart_low = depart.astype(BF16)
        turn = (((1,), (1,)), ((), ()))
        pull = lax.dot_general(depart_low, w2[...], turn, preferred_element_type=F32)
        pull = (pull * (1.0 - active * active)).astype(BF16)
        slope = lax.dot_general(w1[...], pull, turn, preferred_element_type=F32)
        slope = slope + lax.dot_general(sel[...], depart_low, turn, preferred_element_type=F32)
        for n, q in enumerate(tiles):
            for p in range(PLANES):
                for var in range(2):
                    at = p * LANES + var * 64
                    block = slope[at : at + 64, n * LANES : (n + 1) * LANES]
                    mixed[c, pl.ds(var * ROWS + p * NQ + q, 64, stride=2 * ROWS), :] = block


def forward_kernel(
    grid_ref, ids_ref, table_hbm, w1_ref, b1_hbm, w2_ref, b2_hbm, index_hbm, coef_hbm, level_hbm, seen_ref,
    back_ref, lat_ref, lon_ref, rad_ref, cost_ref,
    planes, ids, flip, arrived, mixed, send, got, send_back, back, near_ref, w1raw, w1, w2, obs, sel, strip, turned,
    table_ref, b1_ref, b2_ref, index_ref, coef_ref, level_ref, total,
    grid_sem, ids_sem, table_sem, small_sem, w1_sem, w2_sem, obs_sem, own_sem, out1, in1, out2, in2, out3, in3, out4, in4,
):
    me, peers, (near, near_peers), (far, far_peers) = targets()
    strips = [pl.ds(j * LANES, LANES) for j in range(STRIPS)]
    ids_copies = [pltpu.make_async_copy(ids_ref.at[:, s], ids.at[j], ids_sem.at[j]) for j, s in enumerate(strips)]
    for copy in ids_copies:
        copy.start()
    table_copy = pltpu.make_async_copy(table_hbm, table_ref, table_sem)
    table_copy.start()
    grid_copies = [
        pltpu.make_async_copy(grid_ref.at[p, :, s], planes.at[p, j], grid_sem.at[p, j])
        for p in range(PLANES)
        for j, s in enumerate(strips)
    ]
    for copy in grid_copies:
        copy.start()
    w1_copy = pltpu.make_async_copy(w1_ref, w1raw, w1_sem)
    w2_copy = pltpu.make_async_copy(w2_ref, w2, w2_sem)
    obs_copy = pltpu.make_async_copy(seen_ref, obs, obs_sem)
    small_copies = [
        pltpu.make_async_copy(here, there, small_sem.at[n])
        for n, (here, there) in enumerate(
            (
                (index_hbm, index_ref), (coef_hbm, coef_ref), (level_hbm, level_ref), (b1_hbm, b1_ref), (b2_hbm, b2_ref)
            )
        )
    ]
    for copy in small_copies:
        copy.start()
    w1_copy.start()
    w2_copy.start()
    obs_copy.start()

    barrier = pltpu.get_barrier_semaphore()
    for lev, var in peers:
        pl.semaphore_signal(barrier, 1, device_id=(lev, var), device_id_type=MESH)

    for copy in ids_copies:
        copy.wait()
    table_copy.wait()

    def outward(p):
        def one(lev, var):
            pltpu.make_async_remote_copy(
                send.at[p, lev * 2 + var], got.at[p, me], out1.at[p], in1.at[p],
                device_id=(lev, var), device_id_type=MESH,
            ).start()

        yield from (functools.partial(one, lev, var) for lev, var in peers)
        yield pltpu.make_async_copy(send.at[p, me], got.at[p, me], own_sem.at[p]).start

    def homeward(c):
        def one(lev, var):
            pltpu.make_async_remote_copy(
                send_back.at[c, lev * 2 + var], back.at[c, me], out2.at[c], in2.at[c],
                device_id=(lev, var), device_id_type=MESH,
            ).start()

        yield from (functools.partial(one, lev, var) for lev, var in peers)
        yield pltpu.make_async_copy(send_back.at[c, me], back.at[c, me], own_sem.at[c]).start

    @pl.loop(0, PLANES)
    def _(p):
        for j, s in enumerate(strips):
            pltpu.make_async_copy(grid_ref.at[p, :, s], planes.at[p, j], grid_sem.at[p, j]).wait()
        smooth(p, ids, table_ref, planes, flip, lat_ref, lon_ref, arrived)
        narrow(arrived, p, send)

        @pl.when(p == 0)
        def _():
            pl.semaphore_wait(barrier, DEVICES - 1)

        for start in outward(p):
            start()

    for copy in small_copies:
        copy.wait()
    selection(index_ref, coef_ref, level_ref, sel)
    w1_copy.wait()
    regroup(w1raw, strip, w1)
    w2_copy.wait()
    obs_copy.wait()
    total[...] = jnp.zeros_like(total)
    others = pl.ds(0, DEVICES - 1)

    @pl.loop(0, PLANES)
    def _(p):
        pltpu.make_async_copy(send.at[p, me], got.at[p, me], own_sem.at[p]).wait()
        pltpu.make_async_copy(got.at[p, others], got.at[p, others], in1.at[p]).wait()
        widen(got, p, arrived)

    def chunk(c):
        network(c, arrived, mixed, turned, w1, b1_ref, w2, b2_ref, sel, obs, rad_ref, total)
        narrow(mixed, c, send_back)

    @pl.loop(0, CHUNKS)
    def _(c):
        chunk(c)

        @pl.when(c == CHUNKS - 1)
        def _():
            summed = jnp.sum(total[...], axis=0, keepdims=True)
            near_ref[near] = sum(summed[:, n * LANES : (n + 1) * LANES] for n in range(CHANNELS // LANES))
            for lev, var in near_peers:
                pltpu.make_async_remote_copy(
                    near_ref.at[near], near_ref.at[near], out3, in3, device_id=(lev, var), device_id_type=MESH
                ).start()

        for start in homeward(c):
            start()

    pltpu.make_async_copy(near_ref.at[pl.ds(0, 7)], near_ref.at[pl.ds(0, 7)], out3).wait()
    pltpu.make_async_copy(near_ref.at[pl.ds(0, 7)], near_ref.at[pl.ds(0, 7)], in3).wait()
    cost_ref[far] = jnp.sum(near_ref[...], axis=0)
    for lev, var in far_peers:
        pltpu.make_async_remote_copy(
            cost_ref.at[far], cost_ref.at[far], out4, in4, device_id=(lev, var), device_id_type=MESH
        ).start()
    for c in range(CHUNKS):
        pltpu.make_async_copy(send_back.at[c, me], back.at[c, me], own_sem.at[c]).wait()
        pltpu.make_async_copy(back.at[c, others], back.at[c, others], in2.at[c]).wait()
        widen(back, c, back_ref)
    for c in range(CHUNKS):
        pltpu.make_async_copy(send_back.at[c, others], send_back.at[c, others], out2.at[c]).wait()
    for p in range(PLANES):
        pltpu.make_async_copy(send.at[p, others], send.at[p, others], out1.at[p]).wait()
    pltpu.make_async_copy(cost_ref.at[pl.ds(0, 15)], cost_ref.at[pl.ds(0, 15)], out4).wait()
    pltpu.make_async_copy(cost_ref.at[pl.ds(0, 15)], cost_ref.at[pl.ds(0, 15)], in4).wait()


def unsmooth(p, mixed, flip, lat_ref, lon_ref, staged):
    for k in range(STEP):
        pieces = [
            mixed[c, pl.ds(k * ROWS + p * NQ + q, 8, stride=STEP * ROWS), :]
            for c in range(CHUNKS)
            for q in range(NQ)
        ]
        flip[0, k] = jnp.concatenate(pieces, axis=1)
    for number in range(PASSES):
        held = flip.at[number % 2]
        sub = lax.broadcasted_iota(jnp.int32, (8, LON), 0)
        first = lat_ref[p, 0] * held[0]
        last = lat_ref[p, STEP - 1] * held[STEP - 1]
        below = jnp.where(sub == 0, 0.0, pltpu.roll(last, 1, 0))
        here = first
        for k in range(STEP):
            if k < STEP - 1:
                above = lat_ref[p, k + 1] * held[k + 1]
            else:
                above = jnp.where(sub == 7, 0.0, pltpu.roll(first, 7, 0))
            value = held[k]
            along = lon_ref[p, k] * value
            value = value + (above + below - (here + here)) + (sideways(along) - (along + along))
            below, here = here, above
            if number < PASSES - 1:
                flip[1 - number % 2, k] = value
            else:
                for j in range(STRIPS):
                    staged[p, j, pl.ds(k, 8, stride=STEP), :] = value[:, j * LANES : (j + 1) * LANES]


def unsmooth(p, mixed, flip, lat_ref, lon_ref, staged):
    for k in range(STEP):
        pieces = [
            mixed[c, pl.ds(k * ROWS + p * NQ + q, 8, stride=STEP * ROWS), :]
            for c in range(CHUNKS)
            for q in range(NQ)
        ]
        flip[0, k] = jnp.concatenate(pieces, axis=1)
    for number in range(PASSES):
        held = flip.at[number % 2]
        sub = lax.broadcasted_iota(jnp.int32, (8, LON), 0)
        first = lat_ref[p, 0] * held[0]
        last = lat_ref[p, STEP - 1] * held[STEP - 1]
        below = jnp.where(sub == 0, 0.0, pltpu.roll(last, 1, 0))
        here = first
        for k in range(STEP):
            if k < STEP - 1:
                above = lat_ref[p, k + 1] * held[k + 1]
            else:
                above = jnp.where(sub == 7, 0.0, pltpu.roll(first, 7, 0))
            value = held[k]
            along = lon_ref[p, k] * value
            value = value + (above + below - (here + here)) + (sideways(along) - (along + along))
            below, here = here, above
            if number < PASSES - 1:
                flip[1 - number % 2, k] = value
            else:
                for j in range(STRIPS):
                    staged[p, j, pl.ds(k, 8, stride=STEP), :] = value[:, j * LANES : (j + 1) * LANES]


def adjoint_kernel(
    back_ref, lat_ref, lon_ref, rad_ref, cost_ref,
    grad_ref, rad_out, mean_ref,
    flip, staged, rad_sem, grad_sem,
):
    rad_copy = pltpu.make_async_copy(rad_ref, rad_out, rad_sem)
    rad_copy.start()

    def leaving(p, j):
        strip = pl.ds(j * LANES, LANES)
        return pltpu.make_async_copy(staged.at[p, j], grad_ref.at[p, :, strip], grad_sem.at[p, j])

    @pl.loop(0, PLANES)
    def _(p):
        unsmooth(p, back_ref, flip, lat_ref, lon_ref, staged)
        for j in range(STRIPS):
            leaving(p, j).start()

    mean_ref[0, 0] = jnp.sum(cost_ref[...]) * (0.5 / (LAT * LON * CHANNELS))
    for p in range(PLANES):
        for j in range(STRIPS):
            leaving(p, j).wait()
    rad_copy.wait()


def shards(
    background, field_ids, filter_table, first_weight, first_bias, second_weight, second_bias,
    predictor_index, predictor_coef, channel_level, observed,
):
    vmem = pl.BlockSpec(memory_space=pltpu.VMEM)
    smem = pl.BlockSpec(memory_space=pltpu.SMEM)
    anywhere = pl.BlockSpec(memory_space=pltpu.HBM)
    dma = pltpu.SemaphoreType.DMA
    message = (CHUNKS, DEVICES, ROWS, LANES)
    coefs = jax.ShapeDtypeStruct((PLANES, STEP, 8, LON), F32)
    outcome = pl.pallas_call(
        forward_kernel,
        out_shape=(
            jax.ShapeDtypeStruct((CHUNKS, DEVICES * ROWS, LANES), F32),
            coefs,
            coefs,
            jax.ShapeDtypeStruct((LON, CHANNELS), BF16),
            jax.ShapeDtypeStruct((DEVICES // 8, 1, LANES), F32),
        ),
        in_specs=[anywhere] * 11,
        out_specs=[vmem] * 5,
        scratch_shapes=[
            pltpu.VMEM((PLANES, STRIPS, LAT, LANES), F32),
            pltpu.VMEM((STRIPS, LAT, LANES), jnp.int32),
            pltpu.VMEM((2, STEP, 8, LON), F32),
            pltpu.VMEM((PLANES, DEVICES * STRIPS, LANES), F32),
            pltpu.VMEM((CHUNKS, DEVICES * ROWS, LANES), F32),
            pltpu.VMEM((PLANES, DEVICES, STRIPS, LANES), BF16),
            pltpu.VMEM((PLANES, DEVICES, STRIPS, LANES), BF16),
            pltpu.VMEM(message, BF16),
            pltpu.VMEM(message, BF16),
            pltpu.VMEM((8, 1, LANES), F32),
            pltpu.VMEM((FEATURES, UNITS), BF16),
            pltpu.VMEM((FEATURES, UNITS), BF16),
            pltpu.VMEM((UNITS, CHANNELS), BF16),
            pltpu.VMEM((LON, CHANNELS), F32),
            pltpu.VMEM((FEATURES, CHANNELS), BF16),
            pltpu.VMEM((FEATURES, LANES), F32),
            pltpu.VMEM((FEATURES, BLOCK), F32),
            pltpu.SMEM((PLANES, 2, FIELDS), F32),
            pltpu.VMEM((1, UNITS), F32),
            pltpu.VMEM((1, CHANNELS), F32),
            pltpu.VMEM((TERMS, CHANNELS), jnp.int32),
            pltpu.VMEM((TERMS, CHANNELS), F32),
            pltpu.VMEM((1, CHANNELS), jnp.int32),
            pltpu.VMEM((8, CHANNELS), F32),
            dma((PLANES, STRIPS)), dma((STRIPS,)), dma, dma((5,)), dma, dma, dma,
            dma((PLANES,)), dma((PLANES,)), dma((PLANES,)), dma((CHUNKS,)), dma((CHUNKS,)), dma, dma, dma, dma,
        ],
        compiler_params=pltpu.CompilerParams(
            collective_id=0, has_side_effects=True, vmem_limit_bytes=40 * 1024 * 1024
        ),
    )(
        *(
            pltpu.with_memory_space_constraint(operand, pltpu.HBM)
            for operand in (
                background.reshape(PLANES, LAT, LON),
                field_ids,
                filter_table.transpose(1, 2, 3, 0).reshape(PLANES, 2, FIELDS),
                first_weight,
                first_bias.reshape(1, UNITS),
                second_weight,
                second_bias.reshape(1, CHANNELS),
                predictor_index.T,
                predictor_coef.T,
                channel_level.reshape(1, CHANNELS),
                observed.reshape(LON, CHANNELS),
            )
        )
    )
    gradient, radiances, mean_cost = pl.pallas_call(
        adjoint_kernel,
        out_shape=(
            jax.ShapeDtypeStruct((PLANES, LAT, LON), F32),
            jax.ShapeDtypeStruct((LON, CHANNELS), BF16),
            jax.ShapeDtypeStruct((1, 1), F32),
        ),
        in_specs=[vmem] * 5,
        out_specs=[anywhere, anywhere, smem],
        scratch_shapes=[
            pltpu.VMEM((2, STEP, 8, LON), F32),
            pltpu.VMEM((PLANES, STRIPS, LAT, LANES), F32),
            dma,
            dma((PLANES, STRIPS)),
        ],
        compiler_params=pltpu.CompilerParams(vmem_limit_bytes=24 * 1024 * 1024),
    )(*outcome)
    return (
        radiances.reshape(1, LON, CHANNELS),
        mean_cost.reshape(()),
        gradient.reshape(2, 2, LAT, LON),
    )


def solution(mesh):
    placed = (
        P("lev", "var", None, None), P(), P(None, "lev", "var", None), P(), P(), P(), P(), P(), P(), P(),
        P(("lev", "var"), None, None),
    )
    return jax.shard_map(
        shards,
        mesh=mesh,
        in_specs=placed,
        out_specs=(P(("lev", "var"), None, None), P(), P("lev", "var", None, None)),
        check_vma=False,
    )
```
